256 devices in a mesh: row: 8 (over x, core), col: 32 (over y, z).
Axes of the slice: x: 4, y: 4, z: 8, core: 2. Of those that a mesh axis runs over, the one named last changes fastest.
Arguments:
- hidden: bfloat16 [4096, 8192], P('row', 'col'), may hold values from -600 to 600
- norm_gain: float32 [8192], replicated, may hold values from 0.5 to 2
- wq: bfloat16 [8192, 8192], P('row', 'col'), may hold values from -1 to 1
- wk: bfloat16 [8192, 1024], P('row', 'col'), may hold values from -1 to 1
- wv: bfloat16 [8192, 1024], P('row', 'col'), may hold values from -0.0625 to 0.0625
- wo: bfloat16 [8192, 8192], P('row', 'col'), may hold values from -0.25 to 0.25
Outputs:
- attn_out: bfloat16 [4096, 8192], P('row', 'col')
The draws below stay inside these ranges and needn't reach their ends.
All inputs are finite; a program needn't handle non-finite values.
Results may differ from the reference program's by a relative error of at most 0.011.
Values may be sent and summed in bfloat16 or wider, within the bound.
A program may use at most 64 MiB of HBM per device.

```python
import math
import jax
import jax.numpy as jnp
from jax import lax

D = 8192
H = 64
KVH = 8
HD = 128
TOKENS = 4096


def draw_hidden(key, part):
    first, second = jax.random.split(jax.random.fold_in(key, 11), 2)
    normal = jax.random.truncated_normal(first, -6.0, 6.0, (TOKENS, D), jnp.float32)
    col_scale = jnp.exp(jax.random.uniform(second, (D,), jnp.float32, 0.0, math.log(10.0)))
    field = normal * col_scale[None, :]
    return field.astype(jnp.bfloat16)


def drawn_weight(key, salt, heads):
    normal = jax.random.truncated_normal(jax.random.fold_in(key, salt), -6.0, 6.0, (D, heads * HD), jnp.float32)
    weight = normal * D ** (-0.5)
    return weight


def draw_wq(key, part):
    return drawn_weight(key, 21, H).astype(jnp.bfloat16)


def draw_wk(key, part):
    return drawn_weight(key, 31, KVH).astype(jnp.bfloat16)


def level_of(key, dims, shards, least, high):
    loudness, own = 1.0, jax.random.fold_in(key, 6)
    for axis_at, parts in shards:
        draws = jnp.exp(jax.random.uniform(jax.random.fold_in(own, axis_at), (parts,), jnp.float32, least / len(shards), high / len(shards)))
        loudness = loudness * jnp.repeat(draws, dims[axis_at] // parts).reshape([-1 if axis == axis_at else 1 for axis in range(len(dims))])
    return loudness


def noise(stream_key, shape, spread, reach, pieces=(), kind=jnp.bfloat16):
    drawn = jax.random.normal(stream_key, shape, jnp.float32) * spread
    if len(pieces) > 0:
        drawn = level_of(stream_key, shape, pieces, -0.22, 0.18) * drawn
    return jnp.clip(drawn, min=-reach, max=reach).astype(kind)


def setup_inputs(seed: int = 0) -> dict:
    key_of = jax.random.split(jax.random.key(seed), 7)
    return {
        "hidden": draw_hidden(jax.random.fold_in(key_of[6], 71), 0),
        "norm_gain": jnp.clip(jnp.exp(jax.random.uniform(key_of[1], (D,), jnp.float32, math.log(0.5), math.log(2.0))), 0.5, 2.0),
        "wq": draw_wq(jax.random.fold_in(key_of[6], 71), 0),
        "wk": draw_wk(jax.random.fold_in(key_of[6], 71), 0),
        "wv": noise(key_of[4], (D, KVH * HD), D ** -0.5, 0.0625, ((0, 8), (1, 32))),
        "wo": noise(key_of[5], (H * HD, D), 0.035, 0.25, ((0, 8), (1, 32))),
    }


def rotary(field, positions):
    half = field.shape[-1] // 2
    steps = jnp.arange(half).astype(jnp.float32)
    freqs = 10000.0 ** (-steps / half)
    angles = positions.astype(jnp.float32)[:, None] * freqs[None, :]
    cosine = jnp.cos(angles)[:, None, :]
    sine = jnp.sin(angles)[:, None, :]
    first = field[..., :half]
    second = field[..., half:]
    return jnp.concatenate([first * cosine - second * sine, second * cosine + first * sine], axis=-1)

def reference(hidden, norm_gain, wq, wk, wv, wo):
    values_in = hidden.astype(jnp.float32)
    meansq = lax.optimization_barrier(jnp.mean(values_in * values_in, axis=1, keepdims=True))
    normed = (values_in * lax.rsqrt(meansq + 1e-05) * norm_gain).astype(jnp.bfloat16)
    qraw = jnp.dot(normed, wq, preferred_element_type=jnp.float32)
    kraw = jnp.dot(normed, wk, preferred_element_type=jnp.float32)
    vraw = jnp.dot(normed, wv, preferred_element_type=jnp.float32)
    positions = jnp.arange(TOKENS).astype(jnp.int32)
    queries = rotary(qraw.reshape(TOKENS, H, HD), positions).astype(jnp.bfloat16)
    keys = rotary(kraw.reshape(TOKENS, KVH, HD), positions).astype(jnp.bfloat16)
    values = vraw.reshape(TOKENS, KVH, HD).astype(jnp.bfloat16)
    per_kv = H // KVH
    query_groups = queries.reshape(TOKENS, KVH, per_kv, HD).transpose(1, 2, 0, 3)
    key_groups = keys.transpose(1, 0, 2)
    value_groups = values.transpose(1, 0, 2)
    visible = positions[:, None] >= positions[None, :]
    scale = HD ** (-0.5)

    def one_group(operands):
        query_block, key_block, value_block = operands
        scores = jnp.einsum('gtd,nd->gtn', query_block.astype(jnp.float32), key_block.astype(jnp.float32)) * scale
        scores = jnp.where(visible[None], scores, -jnp.inf)
        top = lax.optimization_barrier(jnp.max(scores, axis=2, keepdims=True))
        probs = jnp.exp(scores - top)
        total = lax.optimization_barrier(jnp.sum(probs, axis=2, keepdims=True))
        rounded = lax.optimization_barrier(probs.astype(jnp.bfloat16)).astype(jnp.float32)
        numer = jnp.einsum('gtn,nd->gtd', rounded, value_block.astype(jnp.float32))
        return (numer / total).astype(jnp.bfloat16)
    outputs = lax.map(one_group, (query_groups, key_groups, value_groups))
    heads = outputs.transpose(2, 0, 1, 3).reshape(TOKENS, H * HD)
    return jnp.dot(heads, wo, preferred_element_type=jnp.float32).astype(jnp.bfloat16)
```

```python
import functools

import jax
import jax.numpy as jnp
from jax import lax
from jax.experimental import pallas as pl
from jax.experimental.pallas import tpu as pltpu
from jax.sharding import PartitionSpec as P

MESH = pl.DeviceIdType.MESH
BF = jnp.bfloat16
F32 = jnp.float32
HD = 128
TOK = 512
HALF = 256
COLS = 256
KROWS = 1024
NX, NY, NZ = 4, 4, 8
D = 8192
EXP2_SCALE = HD ** (-0.5) * 1.4426950408889634


def wait_bytes(ref, sem):
    pltpu.make_async_copy(ref, ref, sem).wait()


def kernel(
    hid, gain, wq, wkv, wo, ctab, stab, out,
    hbuf, wbuf, kvw, wob, acc, kvacc, ssacc, qs, qrx, kvs, kvrx, kvb, ssb, rcol, qb, hb, osb, orx,
    t_s, t_r, z_s, z_r, g_s, g_r, y_s, y_r, yk_s, yk_r, yo_s, yo_r,
    c_s, c_r, loc, q_s, q_r, ss_s, ss_r, k_s, k_r, b_s, b_r, p_s, p_r, o_s, o_r,
):
    row = lax.axis_index("row")
    col = lax.axis_index("col")
    x, core = row // 2, row % 2
    y, z = col // NZ, col % NZ
    g, zq = z // 4, z % 4
    d = 2 * y + core
    prow = row + 1 - 2 * core

    def remote(src, dst, ss, rs, r, c):
        return pltpu.make_async_remote_copy(
            src_ref=src, dst_ref=dst, send_sem=ss, recv_sem=rs, device_id=(r, c), device_id_type=MESH
        )

    zr, zl = 8 * y + (z + 1) % NZ, 8 * y + (z + NZ - 1) % NZ
    yr, yl = 8 * ((y + 1) % NY) + z, 8 * ((y + NY - 1) % NY) + z
    low = row < 4
    t_y = jnp.where(low, row, 7 - row)

    barrier = pltpu.get_barrier_semaphore()

    def greet(r, c):
        pl.semaphore_signal(barrier, inc=1, device_id=(r, c), device_id_type=MESH)

    def greet_maybe_self(r, c):
        me = jnp.logical_and(r == row, c == col)

        @pl.when(jnp.logical_not(me))
        def _():
            greet(r, c)

        return jnp.where(me, 0, 1)

    count = 0
    for c in (zr, zl, yr, yl):
        greet(row, c)
        count += 1
    greet(prow, col)
    count += 1
    count += greet_maybe_self(y, 8 * x + z)
    count += greet_maybe_self(7 - y, 8 * x + z)
    for dx in range(4):
        for dj in range(4):
            if dx or dj:
                greet(2 * ((x + dx) % NX) + core, 8 * y + 4 * g + (zq + dj) % 4)
                count += 1
    for dy in range(1, 4):
        for dj in range(4):
            greet(row, 8 * ((y + dy) % NY) + 4 * g + (zq + dj) % 4)
            count += 1
    for xs in range(4):
        for cs in range(2):
            count += greet_maybe_self(2 * xs + cs, 8 * t_y + z)

    own = [
        pltpu.make_async_copy(wq, wbuf.at[core, y], loc.at[0]),
        pltpu.make_async_copy(wkv, kvw.at[core, :, pl.ds(pl.multiple_of(128 * y, 128), 128)], loc.at[1]),
        pltpu.make_async_copy(wo, wob.at[core, y], loc.at[2]),
    ]
    for c in own:
        c.start()
    acc[...] = jnp.zeros_like(acc)
    kvacc[...] = jnp.zeros_like(kvacc)
    ssacc[...] = jnp.zeros_like(ssacc)
    pl.semaphore_wait(barrier, count)

    t_copies = []
    for h in range(2):
        tcore = jnp.where(low, h, 1 - h)
        slot = jnp.where(low, 0, 1)
        tr, tc = 2 * y + tcore, 8 * t_y + z
        me = jnp.logical_and(tr == row, tc == col)
        src = hid.at[pl.ds(HALF * h, HALF)]
        dst = hbuf.at[z, pl.ds(pl.multiple_of(HALF * slot, HALF), HALF)]
        cp = remote(src, dst, t_s.at[h], t_r.at[slot], tr, tc)
        t_copies.append((cp, me))

        @pl.when(me)
        def _():
            pltpu.make_async_copy(src, dst, t_r.at[slot]).start()

        @pl.when(jnp.logical_not(me))
        def _():
            cp.start()

    sends = []

    def go(cp):
        cp.start()
        sends.append(cp)

    kl = pl.ds(pl.multiple_of(128 * y, 128), 128)
    go(remote(wq, wbuf.at[core, y], y_s.at[0, 0], y_r.at[0, 0], row, yr))
    go(remote(wq, wbuf.at[core, y], y_s.at[1, 0], y_r.at[1, 0], row, yl))
    go(remote(wkv, kvw.at[core, :, kl], yk_s.at[0, 0], yk_r.at[0, 0], row, yr))
    go(remote(wkv, kvw.at[core, :, kl], yk_s.at[1, 0], yk_r.at[1, 0], row, yl))
    go(remote(wq, wbuf.at[core, y], c_s.at[0], c_r.at[0], prow, col))
    go(remote(wkv, kvw.at[core, :, kl], c_s.at[0], c_r.at[1], prow, col))

    def ring_send(buf, ss, rs, s, h):
        hs = pl.ds(HALF * h, HALF)
        a = (z + NZ - s) % NZ
        b = (z + s) % NZ
        if s < 3 or h == 0:
            go(remote(buf.at[a, hs], buf.at[a, hs], ss.at[0, s, h], rs.at[0, s, h], row, zr))
        if s < 3 or h == 1:
            go(remote(buf.at[b, hs], buf.at[b, hs], ss.at[1, s, h], rs.at[1, s, h], row, zl))

    def ring_wait(buf, rs, s, h):
        hs = pl.ds(HALF * h, HALF)
        if s < 3 or h == 0:
            wait_bytes(buf.at[(z + NZ - s - 1) % NZ, hs], rs.at[0, s, h])
        if s < 3 or h == 1:
            wait_bytes(buf.at[(z + s + 1) % NZ, hs], rs.at[1, s, h])

    def ring_step(buf, ss, rs, s):
        for h in range(2):
            ring_wait(buf, rs, s, h)
            if s < 3:
                ring_send(buf, ss, rs, s + 1, h)

    for h in range(2):
        wait_bytes(hbuf.at[z, pl.ds(HALF * h, HALF)], t_r.at[h])
        ring_send(hbuf, z_s, z_r, 0, h)

    ring_step(hbuf, z_s, z_r, 0)

    y1, y3, y2 = (y + 1) % NY, (y + 3) % NY, (y + 2) % NY

    def weight_hop(buf, sems, rsems, c_sem, half_rows):
        wait_bytes(buf.at[core, y3], rsems.at[0, 0])
        go(remote(buf.at[core, y3, pl.ds(0, half_rows)], buf.at[core, y3, pl.ds(0, half_rows)],
                  sems.at[0, 1], rsems.at[0, 1], row, yr))
        wait_bytes(buf.at[core, y1], rsems.at[1, 0])
        go(remote(buf.at[core, y1, pl.ds(half_rows, half_rows)], buf.at[core, y1, pl.ds(half_rows, half_rows)],
                  sems.at[1, 1], rsems.at[1, 1], row, yl))
        for b in (y3, y1):
            go(remote(buf.at[core, b], buf.at[core, b], c_s.at[0], c_sem, prow, col))

    def weight_last(buf, rsems, c_sem, half_rows):
        wait_bytes(buf.at[core, y2, pl.ds(0, half_rows)], rsems.at[0, 1])
        wait_bytes(buf.at[core, y2, pl.ds(half_rows, half_rows)], rsems.at[1, 1])
        go(remote(buf.at[core, y2], buf.at[core, y2], c_s.at[0], c_sem, prow, col))

    def lanes(b):
        return pl.ds(pl.multiple_of(128 * b, 128), 128)

    weight_hop(wbuf, y_s, y_r, c_r.at[0], KROWS // 2)
    l3, l1, l2 = lanes(y3), lanes(y1), lanes(y2)
    top, bot = pl.ds(0, 256), pl.ds(256, 256)
    wait_bytes(kvw.at[core, :, l3], yk_r.at[0, 0])
    go(remote(kvw.at[core, top, l3], kvw.at[core, top, l3], yk_s.at[0, 1], yk_r.at[0, 1], row, yr))
    wait_bytes(kvw.at[core, :, l1], yk_r.at[1, 0])
    go(remote(kvw.at[core, bot, l1], kvw.at[core, bot, l1], yk_s.at[1, 1], yk_r.at[1, 1], row, yl))
    for b in (l3, l1):
        go(remote(kvw.at[core, :, b], kvw.at[core, :, b], c_s.at[0], c_r.at[1], prow, col))

    ring_step(hbuf, z_s, z_r, 1)

    weight_last(wbuf, y_r, c_r.at[0], KROWS // 2)
    wait_bytes(kvw.at[core, top, l2], yk_r.at[0, 1])
    wait_bytes(kvw.at[core, bot, l2], yk_r.at[1, 1])
    go(remote(kvw.at[core, :, l2], kvw.at[core, :, l2], c_s.at[0], c_r.at[1], prow, col))

    go(remote(wo, wob.at[core, y], yo_s.at[0, 0], yo_r.at[0, 0], row, yr))
    go(remote(wo, wob.at[core, y], yo_s.at[1, 0], yo_r.at[1, 0], row, yl))
    go(remote(wo, wob.at[core, y], c_s.at[0], c_r.at[2], prow, col))

    other = 1 - core
    wait_bytes(wbuf.at[other], c_r.at[0])
    wait_bytes(kvw.at[other], c_r.at[1])
    for c in own:
        c.wait()

    lane512 = lax.broadcasted_iota(jnp.int32, (TOK, 512), 1) % 128 // 64

    def project(zi):
        at = pl.multiple_of(2048 * x + COLS * zi, COLS)
        hv = hbuf[zi].astype(F32)
        sq = hv * hv
        ssacc[...] += sq[:, :128] + sq[:, 128:]
        hg = (hv * gain[:, pl.ds(at, COLS)]).astype(BF)
        kr = pl.ds(pl.multiple_of(zi % 4 * 256, 256), 256)
        for b in range(4):
            acc[b] += jnp.dot(hg, wbuf[zi // 4, b, kr, :], preferred_element_type=F32)
        kk = pl.ds(pl.multiple_of(zi % 2 * 256, 256), 256)
        part = jnp.dot(hg, kvw[zi // 4, kk, :], preferred_element_type=F32)
        kvacc[...] += jnp.where(lane512 == zi % 4 // 2, part, 0.0)

    def near(i, _):
        project((z + NZ - 2 + i) % NZ)
        return 0

    lax.fori_loop(0, 5, near, 0)
    ring_step(hbuf, z_s, z_r, 2)

    def far(i, _):
        project((z + 3 + 2 * i) % NZ)
        return 0

    lax.fori_loop(0, 2, far, 0)
    ring_step(hbuf, z_s, z_r, 3)
    project((z + 4) % NZ)

    for dx in range(4):
        xt = (x + dx) % NX
        kvs[dx] = kvacc[:, lanes(xt)].astype(BF)
        for dj in range(4):
            jq = (zq + dj) % 4
            piece = kvs.at[dx, pl.ds(pl.multiple_of(128 * jq, 128), 128)]
            slot = (4 - dx) % 4 * 4 + (4 - dj) % 4
            if slot == 0:
                kvrx[0] = kvs[dx, pl.ds(pl.multiple_of(128 * jq, 128), 128), :]
            else:
                go(remote(piece, kvrx.at[slot], k_s.at[0], k_r.at[0], 2 * xt + core, 8 * y + 4 * g + jq))
    ssb[0] = lax.dot_general(
        jnp.ones((8, 128), F32), ssacc[...], (((1,), (1,)), ((), ())),
        precision=lax.Precision.HIGHEST, preferred_element_type=F32,
    )
    for dx in range(1, 4):
        go(remote(ssb.at[0], ssb.at[dx], ss_s.at[0], ss_r.at[0], 2 * ((x + dx) % NX) + core, col))
    for dx in range(1, 4):
        xt = (x + dx) % NX
        qs[dx - 1] = acc[xt].astype(BF)
        go(remote(qs.at[dx - 1], qrx.at[dx - 1], q_s.at[0], q_r.at[0], 2 * xt + core, col))

    wait_bytes(ssb.at[pl.ds(1, 3)], ss_r.at[0])
    total = ssb[0] + ssb[1] + ssb[2] + ssb[3]
    r8 = lax.rsqrt(total / D + 1e-05)
    rcol[...] = lax.dot_general(
        r8, jnp.full((8, 128), 0.125, F32), (((0,), (0,)), ((), ())),
        precision=lax.Precision.HIGHEST, preferred_element_type=F32,
    )

    wait_bytes(kvrx.at[pl.ds(1, 15)], k_r.at[0])
    mine = pl.ds(pl.multiple_of(128 * zq, 128), 128)
    lane = lax.broadcasted_iota(jnp.int32, (128, 128), 1) // 32
    keys = jnp.zeros((128, 128), F32)
    vals = jnp.zeros((128, 128), F32)
    for j in range(4):
        dj = (j + 4 - zq) % 4
        part = kvrx[dj].astype(F32)
        for dx in range(1, 4):
            part += kvrx[4 * dx + dj].astype(F32)
        part = part + pltpu.roll(part, 64, 1)
        keys = jnp.where(lane == j, part if j % 2 == 0 else pltpu.roll(part, 32, 1), keys)
        vals = jnp.where(lane == j, part if j % 2 == 1 else pltpu.roll(part, 96, 1), vals)
    keys = keys * rcol[mine, :]
    vals = vals * rcol[mine, :]
    keys = keys * ctab[mine, :] + pltpu.roll(keys, 64, 1) * stab[mine, :]

    def block_at(yy, jj):
        dd = 2 * yy + core
        return jnp.where(jj < 2, 2 * dd, 2 * (15 - dd)) + jj % 2

    here = block_at(y, zq)
    kvb[here, :, 0:128] = keys.astype(BF)
    kvb[here, :, 128:256] = vals.astype(BF)
    peers = []
    for dy in range(4):
        for dj in range(4):
            if dy or dj:
                yy, jj = (y + dy) % NY, (zq + dj) % 4
                peers.append((yy, jj))
                go(remote(kvb.at[here], kvb.at[here], b_s.at[0], b_r.at[0], row, 8 * yy + 4 * g + jj))
    go(remote(kvb.at[here], kvb.at[here], p_s.at[0], p_r.at[0], prow, col))

    wait_bytes(qrx, q_r.at[0])
    for h in range(2):
        hl = slice(128 * h, 128 * h + 128)
        q = acc[x, :, hl]
        for i in range(3):
            q += qrx[i, :, hl].astype(F32)
        q = q * rcol[...]
        q = (q * ctab[...] + pltpu.roll(q, 64, 1) * stab[...]).astype(BF)
        for k in range(2):
            qb[k, HALF * h : HALF * (h + 1), :] = q[HALF * k : HALF * (k + 1), :]

    weight_hop(wob, yo_s, yo_r, c_r.at[2], KROWS // 2)

    wait_bytes(kvb.at[pl.ds(0, 15)], b_r.at[0])
    for yy, jj in peers:
        b = block_at(yy, jj)
        go(remote(kvb.at[b], kvb.at[b], p_s.at[0], p_r.at[0], prow, col))
    wait_bytes(kvb.at[pl.ds(0, 16)], p_r.at[0])

    rows = 2 * HALF
    tri = (
        lax.broadcasted_iota(jnp.int32, (rows, HALF), 0) % HALF
        >= lax.broadcasted_iota(jnp.int32, (rows, HALF), 1)
    )

    for k in range(2):
        qk = qb[k]

        def scores(t):
            key = kvb[pl.ds(2 * t, 2), :, 0:128].reshape(HALF, 128)
            val = kvb[pl.ds(2 * t, 2), :, 128:256].reshape(HALF, 128)
            s = lax.dot_general(qk, key, (((1,), (1,)), ((), ())), preferred_element_type=F32)
            return s * EXP2_SCALE, val

        last = d if k == 0 else 15 - d
        s, val = scores(last)
        s = jnp.where(tri, s, -jnp.inf)
        top_ = jnp.max(s, axis=1, keepdims=True)
        p = jnp.exp2(s - top_)
        den = jnp.sum(p, axis=1, keepdims=True)
        num = jnp.dot(p.astype(BF), val, preferred_element_type=F32)

        def step(t, carry):
            top_, den, num = carry
            s, val = scores(t)
            new = jnp.maximum(top_, jnp.max(s, axis=1, keepdims=True))
            fix = jnp.exp2(top_ - new)
            p = jnp.exp2(s - new)
            den = den * fix + jnp.sum(p, axis=1, keepdims=True)
            num = num * fix + jnp.dot(p.astype(BF), val, preferred_element_type=F32)
            return new, den, num

        top_, den, num = lax.fori_loop(0, last, step, (top_, den, num))
        res = (num / den).astype(BF)
        for h in range(2):
            hb[z, HALF * k : HALF * (k + 1), 128 * h : 128 * (h + 1)] = res[HALF * h : HALF * (h + 1), :]
        ring_send(hb, g_s, g_r, 0, k)

    ring_step(hb, g_s, g_r, 0)
    weight_last(wob, yo_r, c_r.at[2], KROWS // 2)
    ring_step(hb, g_s, g_r, 1)
    wait_bytes(wob.at[other], c_r.at[2])
    acc[...] = jnp.zeros_like(acc)

    def finish(zi):
        hg = hb[zi]
        kr = pl.ds(pl.multiple_of(zi % 4 * 256, 256), 256)
        for b in range(4):
            acc[b] += jnp.dot(hg, wob[zi // 4, b, kr, :], preferred_element_type=F32)

    def near_out(i, _):
        finish((z + NZ - 2 + i) % NZ)
        return 0

    lax.fori_loop(0, 5, near_out, 0)
    ring_step(hb, g_s, g_r, 2)

    def far_out(i, _):
        finish((z + 3 + 2 * i) % NZ)
        return 0

    lax.fori_loop(0, 2, far_out, 0)
    ring_step(hb, g_s, g_r, 3)
    finish((z + 4) % NZ)

    o_copies = []
    for b in range(4):
        osb[b] = acc[b].astype(BF)
        for k in range(2):
            tr = y if k == 0 else 7 - y
            ha = core if k == 0 else 1 - core
            me = jnp.logical_and(tr == row, b == y)
            src = osb.at[b, pl.ds(HALF * k, HALF)]
            dst = orx.at[x, ha]
            rs = o_r.at[2 * x + ha]
            cp = remote(src, dst, o_s.at[2 * b + k], rs, tr, 8 * b + z)
            o_copies.append((cp, me))

            @pl.when(me)
            def _():
                pltpu.make_async_copy(src, dst, rs).start()

            @pl.when(jnp.logical_not(me))
            def _():
                cp.start()

    for ha in range(2):
        for xs in range(4):
            wait_bytes(orx.at[xs, ha], o_r.at[2 * xs + ha])
        v = orx[0, ha].astype(F32)
        for xs in range(1, 4):
            v += orx[xs, ha].astype(F32)
        out[HALF * ha : HALF * (ha + 1), :] = v.astype(BF)

    for cp in sends:
        cp.wait_send()
    for cp, me in t_copies + o_copies:

        @pl.when(jnp.logical_not(me))
        def _():
            cp.wait_send()


def per_device(hidden, norm_gain, wq, wk, wv, wo):
    row, col = lax.axis_index("row"), lax.axis_index("col")
    d = 2 * (col // NZ) + row % 2
    i = jnp.arange(TOK)
    positions = jnp.where(i < HALF, HALF * d + i, HALF * (15 - d) + i - HALF)
    steps = jnp.arange(HD // 2).astype(F32)
    freqs = 10000.0 ** (-steps / (HD // 2))
    angles = positions.astype(F32)[:, None] * freqs[None, :]
    cosine, sine = jnp.cos(angles), jnp.sin(angles)
    ctab = jnp.concatenate([cosine, cosine], axis=1)
    stab = jnp.concatenate([-sine, sine], axis=1)
    both = jnp.concatenate([wk, wv], axis=1)
    wkv = jnp.concatenate([both[:512], both[512:]], axis=1)
    dma = pltpu.SemaphoreType.DMA
    vmem = pl.BlockSpec(memory_space=pltpu.VMEM)
    anyw = pl.BlockSpec(memory_space=pl.ANY)
    scratch = [
        pltpu.VMEM((NZ, TOK, COLS), BF),
        pltpu.VMEM((2, NY, KROWS, COLS), BF),
        pltpu.VMEM((2, 512, 512), BF),
        pltpu.VMEM((2, NY, KROWS, COLS), BF),
        pltpu.VMEM((NY, TOK, COLS), F32),
        pltpu.VMEM((TOK, 512), F32),
        pltpu.VMEM((TOK, 128), F32),
        pltpu.VMEM((3, TOK, COLS), BF),
        pltpu.VMEM((3, TOK, COLS), BF),
        pltpu.VMEM((4, TOK, 128), BF),
        pltpu.VMEM((16, 128, 128), BF),
        pltpu.VMEM((32, 128, 256), BF),
        pltpu.VMEM((4, 8, TOK), F32),
        pltpu.VMEM((TOK, 128), F32),
        pltpu.VMEM((2, TOK, 128), BF),
        pltpu.VMEM((NZ, TOK, COLS), BF),
        pltpu.VMEM((NY, TOK, COLS), BF),
        pltpu.VMEM((4, 2, HALF, COLS), BF),
        dma((2,)), dma((2,)),
        dma((2, 4, 2)), dma((2, 4, 2)),
        dma((2, 4, 2)), dma((2, 4, 2)),
        dma((2, 2)), dma((2, 2)),
        dma((2, 2)), dma((2, 2)),
        dma((2, 2)), dma((2, 2)),
        dma((1,)), dma((3,)),
        dma((3,)),
        dma((1,)), dma((1,)),
        dma((1,)), dma((1,)),
        dma((1,)), dma((1,)),
        dma((1,)), dma((1,)),
        dma((1,)), dma((1,)),
        dma((8,)), dma((8,)),
    ]
    return pl.pallas_call(
        kernel,
        out_shape=jax.ShapeDtypeStruct((TOK, COLS), BF),
        in_specs=[anyw, vmem, anyw, anyw, anyw, vmem, vmem],
        out_specs=vmem,
        scratch_shapes=scratch,
        compiler_params=pltpu.CompilerParams(
            collective_id=0, has_side_effects=True, vmem_limit_bytes=56 * 1024 * 1024
        ),
    )(hidden, norm_gain.reshape(1, D), wq, wkv, wo, ctab, stab)


def solution(mesh):
    spec = P("row", "col")
    return jax.shard_map(
        per_device, mesh=mesh, in_specs=(spec, P(), spec, spec, spec, spec), out_specs=spec, check_vma=False
    )
```

```python
import functools

import jax
import jax.numpy as jnp
from jax import lax
from jax.experimental import pallas as pl
from jax.experimental.pallas import tpu as pltpu
from jax.sharding import PartitionSpec as P

MESH = pl.DeviceIdType.MESH
BF = jnp.bfloat16
F32 = jnp.float32
HD = 128
TOK = 512
HALF = 256
COLS = 256
KROWS = 1024
NX, NY, NZ = 4, 4, 8
D = 8192
EXP2_SCALE = HD ** (-0.5) * 1.4426950408889634


def wait_bytes(ref, sem):
    pltpu.make_async_copy(ref, ref, sem).wait()


def kernel(
    hid, gain, wq, wkv, wo, ctab, stab, out,
    hbuf, wbuf, kvw, wob, acc, kvacc, ssacc, qs, qrx, kvs, kvrx, kvb, ssb, rcol, qb, hb, osb, orx, fin, frx,
    t_s, t_r, z_s, z_r, g_s, g_r, y_s, y_r, yk_s, yk_r, yo_s, yo_r,
    c_s, c_r, loc, q_s, q_r, ss_s, ss_r, k_s, k_r, b_s, b_r, bl_r, br_r, bf_r, p_s, p_r, o_s, o_r, f_s, f_r,
):
    row = lax.axis_index("row")
    col = lax.axis_index("col")
    x, core = row // 2, row % 2
    y, z = col // NZ, col % NZ
    g, zq = z // 4, z % 4
    d = 2 * y + core
    prow = row + 1 - 2 * core

    def remote(src, dst, ss, rs, r, c):
        return pltpu.make_async_remote_copy(
            src_ref=src, dst_ref=dst, send_sem=ss, recv_sem=rs, device_id=(r, c), device_id_type=MESH
        )

    zr, zl = 8 * y + (z + 1) % NZ, 8 * y + (z + NZ - 1) % NZ
    yr, yl = 8 * ((y + 1) % NY) + z, 8 * ((y + NY - 1) % NY) + z
    low = row < 4
    t_y = jnp.where(low, row, 7 - row)

    barrier = pltpu.get_barrier_semaphore()

    def greet(r, c):
        pl.semaphore_signal(barrier, inc=1, device_id=(r, c), device_id_type=MESH)

    def greet_maybe_self(r, c):
        me = jnp.logical_and(r == row, c == col)

        @pl.when(jnp.logical_not(me))
        def _():
            greet(r, c)

        return jnp.where(me, 0, 1)

    count = 0
    for c in (zr, zl, yr, yl):
        greet(row, c)
        count += 1
    greet(prow, col)
    count += 1
    count += greet_maybe_self(y, 8 * x + z)
    count += greet_maybe_self(7 - y, 8 * x + z)
    for dx in range(4):
        for dj in range(4):
            if dx or dj:
                greet(2 * ((x + dx) % NX) + core, 8 * y + 4 * g + (zq + dj) % 4)
                count += 1
    for cs in range(2):
        count += greet_maybe_self(2 * y + cs, 8 * t_y + z)

    own = [
        pltpu.make_async_copy(wq, wbuf.at[core, y], loc.at[0]),
        pltpu.make_async_copy(wkv, kvw.at[core, :, pl.ds(pl.multiple_of(128 * y, 128), 128)], loc.at[1]),
        pltpu.make_async_copy(wo, wob.at[core, y], loc.at[2]),
    ]
    for c in own:
        c.start()
    acc[...] = jnp.zeros_like(acc)
    kvacc[...] = jnp.zeros_like(kvacc)
    ssacc[...] = jnp.zeros_like(ssacc)
    pl.semaphore_wait(barrier, count)

    t_copies = []
    for h in range(2):
        tcore = jnp.where(low, h, 1 - h)
        slot = jnp.where(low, 0, 1)
        tr, tc = 2 * y + tcore, 8 * t_y + z
        me = jnp.logical_and(tr == row, tc == col)
        src = hid.at[pl.ds(HALF * h, HALF)]
        dst = hbuf.at[z, pl.ds(pl.multiple_of(HALF * slot, HALF), HALF)]
        cp = remote(src, dst, t_s.at[h], t_r.at[slot], tr, tc)
        t_copies.append((cp, me))

        @pl.when(me)
        def _():
            pltpu.make_async_copy(src, dst, t_r.at[slot]).start()

        @pl.when(jnp.logical_not(me))
        def _():
            cp.start()

    sends = []

    def go(cp):
        cp.start()
        sends.append(cp)

    kl = pl.ds(pl.multiple_of(128 * y, 128), 128)
    go(remote(wq, wbuf.at[core, y], y_s.at[0, 0], y_r.at[0, 0], row, yr))
    go(remote(wq, wbuf.at[core, y], y_s.at[1, 0], y_r.at[1, 0], row, yl))
    go(remote(wkv, kvw.at[core, :, kl], yk_s.at[0, 0], yk_r.at[0, 0], row, yr))
    go(remote(wkv, kvw.at[core, :, kl], yk_s.at[1, 0], yk_r.at[1, 0], row, yl))
    go(remote(wq, wbuf.at[core, y], c_s.at[0], c_r.at[0], prow, col))
    go(remote(wkv, kvw.at[core, :, kl], c_s.at[0], c_r.at[1], prow, col))

    def ring_send(buf, ss, rs, s, h):
        hs = pl.ds(HALF * h, HALF)
        a = (z + NZ - s) % NZ
        b = (z + s) % NZ
        if s < 3 or h == 0:
            go(remote(buf.at[a, hs], buf.at[a, hs], ss.at[0, s, h], rs.at[0, s, h], row, zr))
        if s < 3 or h == 1:
            go(remote(buf.at[b, hs], buf.at[b, hs], ss.at[1, s, h], rs.at[1, s, h], row, zl))

    def ring_wait(buf, rs, s, h):
        hs = pl.ds(HALF * h, HALF)
        if s < 3 or h == 0:
            wait_bytes(buf.at[(z + NZ - s - 1) % NZ, hs], rs.at[0, s, h])
        if s < 3 or h == 1:
            wait_bytes(buf.at[(z + s + 1) % NZ, hs], rs.at[1, s, h])

    def ring_step(buf, ss, rs, s, h):
        ring_wait(buf, rs, s, h)
        if s < 3:
            ring_send(buf, ss, rs, s + 1, h)

    for h in range(2):
        wait_bytes(hbuf.at[z, pl.ds(HALF * h, HALF)], t_r.at[h])
        ring_send(hbuf, z_s, z_r, 0, h)

    ring_step(hbuf, z_s, z_r, 0, 0)

    y1, y3, y2 = (y + 1) % NY, (y + 3) % NY, (y + 2) % NY

    def weight_hop(buf, sems, rsems, c_sem, half_rows):
        wait_bytes(buf.at[core, y3], rsems.at[0, 0])
        go(remote(buf.at[core, y3, pl.ds(0, half_rows)], buf.at[core, y3, pl.ds(0, half_rows)],
                  sems.at[0, 1], rsems.at[0, 1], row, yr))
        wait_bytes(buf.at[core, y1], rsems.at[1, 0])
        go(remote(buf.at[core, y1, pl.ds(half_rows, half_rows)], buf.at[core, y1, pl.ds(half_rows, half_rows)],
                  sems.at[1, 1], rsems.at[1, 1], row, yl))
        for b in (y3, y1):
            go(remote(buf.at[core, b], buf.at[core, b], c_s.at[0], c_sem, prow, col))

    def weight_last(buf, rsems, c_sem, half_rows):
        wait_bytes(buf.at[core, y2, pl.ds(0, half_rows)], rsems.at[0, 1])
        wait_bytes(buf.at[core, y2, pl.ds(half_rows, half_rows)], rsems.at[1, 1])
        go(remote(buf.at[core, y2], buf.at[core, y2], c_s.at[0], c_sem, prow, col))

    def lanes(b):
        return pl.ds(pl.multiple_of(128 * b, 128), 128)

    weight_hop(wbuf, y_s, y_r, c_r.at[0], KROWS // 2)
    ring_step(hbuf, z_s, z_r, 1, 0)
    ring_step(hbuf, z_s, z_r, 0, 1)
    l3, l1, l2 = lanes(y3), lanes(y1), lanes(y2)
    top, bot = pl.ds(0, 256), pl.ds(256, 256)
    wait_bytes(kvw.at[core, :, l3], yk_r.at[0, 0])
    go(remote(kvw.at[core, top, l3], kvw.at[core, top, l3], yk_s.at[0, 1], yk_r.at[0, 1], row, yr))
    wait_bytes(kvw.at[core, :, l1], yk_r.at[1, 0])
    go(remote(kvw.at[core, bot, l1], kvw.at[core, bot, l1], yk_s.at[1, 1], yk_r.at[1, 1], row, yl))
    for b in (l3, l1):
        go(remote(kvw.at[core, :, b], kvw.at[core, :, b], c_s.at[0], c_r.at[1], prow, col))

    ring_step(hbuf, z_s, z_r, 2, 0)
    ring_step(hbuf, z_s, z_r, 1, 1)

    weight_last(wbuf, y_r, c_r.at[0], KROWS // 2)
    wait_bytes(kvw.at[core, top, l2], yk_r.at[0, 1])
    wait_bytes(kvw.at[core, bot, l2], yk_r.at[1, 1])
    go(remote(kvw.at[core, :, l2], kvw.at[core, :, l2], c_s.at[0], c_r.at[1], prow, col))

    go(remote(wo, wob.at[core, y], yo_s.at[0, 0], yo_r.at[0, 0], row, yr))
    go(remote(wo, wob.at[core, y], yo_s.at[1, 0], yo_r.at[1, 0], row, yl))
    go(remote(wo, wob.at[core, y], c_s.at[0], c_r.at[2], prow, col))

    other = 1 - core
    ring_step(hbuf, z_s, z_r, 3, 0)
    ring_step(hbuf, z_s, z_r, 2, 1)
    wait_bytes(wbuf.at[other], c_r.at[0])
    wait_bytes(kvw.at[other], c_r.at[1])
    for c in own:
        c.wait()

    lane512 = lax.broadcasted_iota(jnp.int32, (HALF, 512), 1) % 128 // 64

    def project(zi, h):
        hs = pl.ds(HALF * h, HALF)
        at = pl.multiple_of(2048 * x + COLS * zi, COLS)
        hv = hbuf[zi, hs].astype(F32)
        sq = hv * hv
        ssacc[hs] += sq[:, :128] + sq[:, 128:]
        hg = (hv * gain[:, pl.ds(at, COLS)]).astype(BF)
        kr = pl.ds(pl.multiple_of(zi % 4 * 256, 256), 256)
        for b in range(4):
            acc[b, hs] += jnp.dot(hg, wbuf[zi // 4, b, kr, :], preferred_element_type=F32)
        kk = pl.ds(pl.multiple_of(zi % 2 * 256, 256), 256)
        part = jnp.dot(hg, kvw[zi // 4, kk, :], preferred_element_type=F32)
        kvacc[hs] += jnp.where(lane512 == zi % 4 // 2, part, 0.0)

    k_copies = []

    def reduce_kv(h):
        hs = pl.ds(HALF * h, HALF)
        for dx in range(4):
            xt = (x + dx) % NX
            kvs[dx, hs] = kvacc[hs, lanes(xt)].astype(BF)
            for jq in (2 * h, 2 * h + 1):
                piece = kvs.at[dx, pl.ds(128 * jq, 128)]
                dst = kvrx.at[(4 - dx) % 4 * 4 + (zq + 4 - jq) % 4]
                cp = remote(piece, dst, k_s.at[0], k_r.at[0], 2 * xt + core, 8 * y + 4 * g + jq)
                if dx:
                    go(cp)
                else:
                    me = zq == jq
                    k_copies.append((cp, me))

                    @pl.when(me)
                    def _():
                        pltpu.make_async_copy(piece, dst, k_r.at[0]).start()

                    @pl.when(jnp.logical_not(me))
                    def _():
                        cp.start()

    def reduce_q(h):
        hs = pl.ds(HALF * h, HALF)
        for dx in range(1, 4):
            xt = (x + dx) % NX
            qs[dx - 1, hs] = acc[xt, hs].astype(BF)
            go(remote(qs.at[dx - 1, hs], qrx.at[dx - 1, hs], q_s.at[0], q_r.at[0], 2 * xt + core, col))

    def first_half(i, _):
        project(i, 0)
        return 0

    def second_half(i, _):
        project((z + NZ - 3 + i) % NZ, 1)
        return 0

    lax.fori_loop(0, NZ, first_half, 0)
    reduce_kv(0)
    reduce_q(0)
    weight_hop(wob, yo_s, yo_r, c_r.at[2], KROWS // 2)
    lax.fori_loop(0, 7, second_half, 0)
    ring_step(hbuf, z_s, z_r, 3, 1)
    project((z + 4) % NZ, 1)
    reduce_kv(1)
    ssb[0] = lax.dot_general(
        jnp.ones((8, 128), F32), ssacc[...], (((1,), (1,)), ((), ())),
        precision=lax.Precision.HIGHEST, preferred_element_type=F32,
    )
    for dx in range(1, 4):
        go(remote(ssb.at[0], ssb.at[dx], ss_s.at[0], ss_r.at[0], 2 * ((x + dx) % NX) + core, col))
    reduce_q(1)

    wait_bytes(ssb.at[pl.ds(1, 3)], ss_r.at[0])
    total = ssb[0] + ssb[1] + ssb[2] + ssb[3]
    r8 = lax.rsqrt(total / D + 1e-05)
    rcol[...] = lax.dot_general(
        r8, jnp.full((8, 128), 0.125, F32), (((0,), (0,)), ((), ())),
        precision=lax.Precision.HIGHEST, preferred_element_type=F32,
    )

    wait_bytes(kvrx, k_r.at[0])
    mine = pl.ds(pl.multiple_of(128 * zq, 128), 128)
    lane = lax.broadcasted_iota(jnp.int32, (128, 128), 1) // 32
    keys = jnp.zeros((128, 128), F32)
    vals = jnp.zeros((128, 128), F32)
    for j in range(4):
        dj = (j + 4 - zq) % 4
        part = kvrx[dj].astype(F32)
        for dx in range(1, 4):
            part += kvrx[4 * dx + dj].astype(F32)
        part = part + pltpu.roll(part, 64, 1)
        keys = jnp.where(lane == j, part if j % 2 == 0 else pltpu.roll(part, 32, 1), keys)
        vals = jnp.where(lane == j, part if j % 2 == 1 else pltpu.roll(part, 96, 1), vals)
    keys = keys * rcol[mine, :]
    vals = vals * rcol[mine, :]
    keys = keys * ctab[mine, :] + pltpu.roll(keys, 64, 1) * stab[mine, :]

    def block_at(yy, jj):
        dd = 2 * yy + core
        return jnp.where(jj < 2, 2 * dd, 2 * (15 - dd)) + jj % 2

    here = block_at(y, zq)
    kvb[here, :, 0:128] = keys.astype(BF)
    kvb[here, :, 128:256] = vals.astype(BF)
    kv_here = [block_at(y, (zq + dj) % 4) for dj in range(4)]
    kv_left = [block_at(y3, (zq + dj) % 4) for dj in range(4)]
    kv_right = [block_at(y1, (zq + dj) % 4) for dj in range(4)]
    kv_far = [block_at(y2, (zq + dj) % 4) for dj in range(4)]
    half0, half1 = pl.ds(0, 64), pl.ds(64, 64)

    def to_partner(b):
        go(remote(kvb.at[b], kvb.at[b], p_s.at[0], p_r.at[0], prow, col))

    def kv_hop(dj):
        b = kv_here[dj]
        go(remote(kvb.at[b], kvb.at[b], b_s.at[0], bl_r.at[dj], row, yr))
        go(remote(kvb.at[b], kvb.at[b], b_s.at[0], br_r.at[dj], row, yl))
        to_partner(b)

    for dj in (1, 3, 2):
        go(remote(kvb.at[here], kvb.at[here], b_s.at[0], b_r.at[4 - dj], row, 8 * y + 4 * g + (zq + dj) % 4))
    kv_hop(0)
    for dj in (1, 3, 2):
        wait_bytes(kvb.at[kv_here[dj]], b_r.at[dj])
        kv_hop(dj)
    for dj in (0, 1, 3, 2):
        left, right = kv_left[dj], kv_right[dj]
        wait_bytes(kvb.at[left], bl_r.at[dj])
        go(remote(kvb.at[left, half0], kvb.at[left, half0], b_s.at[0], bf_r.at[0, dj], row, yr))
        wait_bytes(kvb.at[right], br_r.at[dj])
        go(remote(kvb.at[right, half1], kvb.at[right, half1], b_s.at[0], bf_r.at[1, dj], row, yl))
        to_partner(left)
        to_partner(right)

    wait_bytes(qrx, q_r.at[0])
    for h in range(2):
        hl = slice(128 * h, 128 * h + 128)
        q = acc[x, :, hl]
        for i in range(3):
            q += qrx[i, :, hl].astype(F32)
        q = q * rcol[...]
        q = (q * ctab[...] + pltpu.roll(q, 64, 1) * stab[...]).astype(BF)
        for k in range(2):
            qb[k, HALF * h : HALF * (h + 1), :] = q[HALF * k : HALF * (k + 1), :]


    for dj in (0, 1, 3, 2):
        far = kv_far[dj]
        wait_bytes(kvb.at[far, half0], bf_r.at[0, dj])
        wait_bytes(kvb.at[far, half1], bf_r.at[1, dj])
        to_partner(far)
    wait_bytes(kvb.at[pl.ds(0, 16)], p_r.at[0])

    rows = 2 * HALF
    tri = (
        lax.broadcasted_iota(jnp.int32, (rows, HALF), 0) % HALF
        >= lax.broadcasted_iota(jnp.int32, (rows, HALF), 1)
    )

    for k in range(2):
        qk = qb[k]

        def scores(t):
            key = kvb[pl.ds(2 * t, 2), :, 0:128].reshape(HALF, 128)
            val = kvb[pl.ds(2 * t, 2), :, 128:256].reshape(HALF, 128)
            s = lax.dot_general(qk, key, (((1,), (1,)), ((), ())), preferred_element_type=F32)
            return s * EXP2_SCALE, val

        last = d if k == 0 else 15 - d
        s, val = scores(last)
        s = jnp.where(tri, s, -jnp.inf)
        top_ = jnp.max(s, axis=1, keepdims=True)
        p = jnp.exp2(s - top_)
        den = jnp.sum(p, axis=1, keepdims=True)
        num = jnp.dot(p.astype(BF), val, preferred_element_type=F32)

        def step(t, carry):
            top_, den, num = carry
            s, val = scores(t)
            new = jnp.maximum(top_, jnp.max(s, axis=1, keepdims=True))
            fix = jnp.exp2(top_ - new)
            p = jnp.exp2(s - new)
            den = den * fix + jnp.sum(p, axis=1, keepdims=True)
            num = num * fix + jnp.dot(p.astype(BF), val, preferred_element_type=F32)
            return new, den, num

        top_, den, num = lax.fori_loop(0, last, step, (top_, den, num))
        res = (num / den).astype(BF)
        for h in range(2):
            hb[z, HALF * k : HALF * (k + 1), 128 * h : 128 * (h + 1)] = res[HALF * h : HALF * (h + 1), :]
        ring_send(hb, g_s, g_r, 0, k)

    ring_step(hb, g_s, g_r, 0, 0)
    ring_step(hb, g_s, g_r, 1, 0)
    ring_step(hb, g_s, g_r, 0, 1)
    weight_last(wob, yo_r, c_r.at[2], KROWS // 2)
    ring_step(hb, g_s, g_r, 2, 0)
    ring_step(hb, g_s, g_r, 1, 1)
    wait_bytes(wob.at[other], c_r.at[2])
    ring_step(hb, g_s, g_r, 3, 0)
    ring_step(hb, g_s, g_r, 2, 1)
    acc[...] = jnp.zeros_like(acc)

    def finish(zi, h):
        hs = pl.ds(HALF * h, HALF)
        hg = hb[zi, hs]
        kr = pl.ds(pl.multiple_of(zi % 4 * 256, 256), 256)
        for b in range(4):
            acc[b, hs] += jnp.dot(hg, wob[zi // 4, b, kr, :], preferred_element_type=F32)

    def first_out(i, _):
        finish(i, 0)
        return 0

    def second_out(i, _):
        finish((z + NZ - 3 + i) % NZ, 1)
        return 0

    def reduce_out(h):
        hs = pl.ds(HALF * h, HALF)
        for dx in range(1, 4):
            xt = (x + dx) % NX
            osb[dx - 1, hs] = acc[xt, hs].astype(BF)
            go(remote(osb.at[dx - 1, hs], orx.at[dx - 1, hs], o_s.at[h], o_r.at[h], 2 * xt + core, col))

    o_copies = []

    def deliver(h):
        hs = pl.ds(HALF * h, HALF)
        wait_bytes(orx.at[:, hs], o_r.at[h])
        v = acc[x, hs]
        for i in range(3):
            v += orx[i, hs].astype(F32)
        fin[h] = v.astype(BF)
        tr = y if h == 0 else 7 - y
        ha = core if h == 0 else 1 - core
        me = jnp.logical_and(tr == row, x == y)
        src, dst, rs = fin.at[h], frx.at[ha], f_r.at[ha]
        cp = remote(src, dst, f_s.at[h], rs, tr, 8 * x + z)
        o_copies.append((cp, me))

        @pl.when(me)
        def _():
            pltpu.make_async_copy(src, dst, rs).start()

        @pl.when(jnp.logical_not(me))
        def _():
            cp.start()

    lax.fori_loop(0, NZ, first_out, 0)
    reduce_out(0)
    lax.fori_loop(0, 7, second_out, 0)
    ring_step(hb, g_s, g_r, 3, 1)
    finish((z + 4) % NZ, 1)
    reduce_out(1)
    deliver(0)
    deliver(1)
    for ha in range(2):
        wait_bytes(frx.at[ha], f_r.at[ha])
        out[HALF * ha : HALF * (ha + 1), :] = frx[ha]

    for cp in sends:
        cp.wait_send()
    for cp, me in t_copies + k_copies + o_copies:

        @pl.when(jnp.logical_not(me))
        def _():
            cp.wait_send()


def per_device(hidden, norm_gain, wq, wk, wv, wo):
    row, col = lax.axis_index("row"), lax.axis_index("col")
    d = 2 * (col // NZ) + row % 2
    i = jnp.arange(TOK)
    positions = jnp.where(i < HALF, HALF * d + i, HALF * (15 - d) + i - HALF)
    steps = jnp.arange(HD // 2).astype(F32)
    freqs = 10000.0 ** (-steps / (HD // 2))
    angles = positions.astype(F32)[:, None] * freqs[None, :]
    cosine, sine = jnp.cos(angles), jnp.sin(angles)
    ctab = jnp.concatenate([cosine, cosine], axis=1)
    stab = jnp.concatenate([-sine, sine], axis=1)
    both = jnp.concatenate([wk, wv], axis=1)
    wkv = jnp.concatenate([both[:512], both[512:]], axis=1)
    dma = pltpu.SemaphoreType.DMA
    vmem = pl.BlockSpec(memory_space=pltpu.VMEM)
    anyw = pl.BlockSpec(memory_space=pl.ANY)
    scratch = [
        pltpu.VMEM((NZ, TOK, COLS), BF),
        pltpu.VMEM((2, NY, KROWS, COLS), BF),
        pltpu.VMEM((2, 512, 512), BF),
        pltpu.VMEM((2, NY, KROWS, COLS), BF),
        pltpu.VMEM((NY, TOK, COLS), F32),
        pltpu.VMEM((TOK, 512), F32),
        pltpu.VMEM((TOK, 128), F32),
        pltpu.VMEM((3, TOK, COLS), BF),
        pltpu.VMEM((3, TOK, COLS), BF),
        pltpu.VMEM((4, TOK, 128), BF),
        pltpu.VMEM((16, 128, 128), BF),
        pltpu.VMEM((32, 128, 256), BF),
        pltpu.VMEM((4, 8, TOK), F32),
        pltpu.VMEM((TOK, 128), F32),
        pltpu.VMEM((2, TOK, 128), BF),
        pltpu.VMEM((NZ, TOK, COLS), BF),
        pltpu.VMEM((3, TOK, COLS), BF),
        pltpu.VMEM((3, TOK, COLS), BF),
        pltpu.VMEM((2, HALF, COLS), BF),
        pltpu.VMEM((2, HALF, COLS), BF),
        dma((2,)), dma((2,)),
        dma((2, 4, 2)), dma((2, 4, 2)),
        dma((2, 4, 2)), dma((2, 4, 2)),
        dma((2, 2)), dma((2, 2)),
        dma((2, 2)), dma((2, 2)),
        dma((2, 2)), dma((2, 2)),
        dma((1,)), dma((3,)),
        dma((3,)),
        dma((1,)), dma((1,)),
        dma((1,)), dma((1,)),
        dma((1,)), dma((1,)),
        dma((1,)), dma((4,)), dma((4,)), dma((4,)), dma((2, 4)),
        dma((1,)), dma((1,)),
        dma((2,)), dma((2,)),
        dma((2,)), dma((2,)),
    ]
    return pl.pallas_call(
        kernel,
        out_shape=jax.ShapeDtypeStruct((TOK, COLS), BF),
        in_specs=[anyw, vmem, anyw, anyw, anyw, vmem, vmem],
        out_specs=vmem,
        scratch_shapes=scratch,
        compiler_params=pltpu.CompilerParams(
            collective_id=0, has_side_effects=True, vmem_limit_bytes=56 * 1024 * 1024
        ),
    )(hidden, norm_gain.reshape(1, D), wq, wkv, wo, ctab, stab)


def solution(mesh):
    spec = P("row", "col")
    return jax.shard_map(
        per_device, mesh=mesh, in_specs=(spec, P(), spec, spec, spec, spec), out_specs=spec, check_vma=False
    )
```

```python
import functools

import jax
import jax.numpy as jnp
from jax import lax
from jax.experimental import pallas as pl
from jax.experimental.pallas import tpu as pltpu
from jax.sharding import PartitionSpec as P

MESH = pl.DeviceIdType.MESH
BF = jnp.bfloat16
F32 = jnp.float32
HD = 128
TOK = 512
HALF = 256
COLS = 256
KROWS = 1024
NX, NY, NZ = 4, 4, 8
D = 8192
EXP2_SCALE = HD ** (-0.5) * 1.4426950408889634


def wait_bytes(ref, sem):
    pltpu.make_async_copy(ref, ref, sem).wait()


def kernel(
    hid, gain, wq, wkv, wo, ctab, stab, out,
    hbuf, wbuf, kvw, wob, acc, kvacc, ssacc, qs, qrx, kvs, kvrx, kvb, ssb, rcol, qb, hb, osb, orx, fin, frx,
    t_s, t_r, z_s, z_r, g_s, g_r, y_s, y_r, yk_s, yk_r, yo_s, yo_r,
    c_s, c_r, loc, q_s, q_r, ss_s, ss_r, k_s, k_r, b_s, b_r, bl_r, br_r, bf_r, p_s, p_r, o_s, o_r, f_s, f_r,
):
    row = lax.axis_index("row")
    col = lax.axis_index("col")
    x, core = row // 2, row % 2
    y, z = col // NZ, col % NZ
    g, zq = z // 4, z % 4
    d = 2 * y + core
    prow = row + 1 - 2 * core

    def remote(src, dst, ss, rs, r, c):
        return pltpu.make_async_remote_copy(
            src_ref=src, dst_ref=dst, send_sem=ss, recv_sem=rs, device_id=(r, c), device_id_type=MESH
        )

    zr, zl = 8 * y + (z + 1) % NZ, 8 * y + (z + NZ - 1) % NZ
    yr, yl = 8 * ((y + 1) % NY) + z, 8 * ((y + NY - 1) % NY) + z
    low = row < 4
    t_y = jnp.where(low, row, 7 - row)

    barrier = pltpu.get_barrier_semaphore()

    def greet(r, c):
        pl.semaphore_signal(barrier, inc=1, device_id=(r, c), device_id_type=MESH)

    def greet_maybe_self(r, c):
        me = jnp.logical_and(r == row, c == col)

        @pl.when(jnp.logical_not(me))
        def _():
            greet(r, c)

        return jnp.where(me, 0, 1)

    count = 0
    for c in (zr, zl, yr, yl):
        greet(row, c)
        count += 1
    greet(prow, col)
    count += 1
    count += greet_maybe_self(y, 8 * x + z)
    count += greet_maybe_self(7 - y, 8 * x + z)
    for dx in range(4):
        for dj in range(4):
            if dx or dj:
                greet(2 * ((x + dx) % NX) + core, 8 * y + 4 * g + (zq + dj) % 4)
                count += 1
    for cs in range(2):
        count += greet_maybe_self(2 * y + cs, 8 * t_y + z)

    own = [
        pltpu.make_async_copy(wq, wbuf.at[core, y], loc.at[0]),
        pltpu.make_async_copy(wkv, kvw.at[core, :, pl.ds(pl.multiple_of(128 * y, 128), 128)], loc.at[1]),
        pltpu.make_async_copy(wo, wob.at[core, y], loc.at[2]),
    ]
    for c in own:
        c.start()
    acc[...] = jnp.zeros_like(acc)
    kvacc[...] = jnp.zeros_like(kvacc)
    ssacc[...] = jnp.zeros_like(ssacc)
    pl.semaphore_wait(barrier, count)

    t_copies = []
    for h in range(2):
        tcore = jnp.where(low, h, 1 - h)
        slot = jnp.where(low, 0, 1)
        tr, tc = 2 * y + tcore, 8 * t_y + z
        me = jnp.logical_and(tr == row, tc == col)
        src = hid.at[pl.ds(HALF * h, HALF)]
        dst = hbuf.at[z, pl.ds(pl.multiple_of(HALF * slot, HALF), HALF)]
        cp = remote(src, dst, t_s.at[h], t_r.at[slot], tr, tc)
        t_copies.append((cp, me))

        @pl.when(me)
        def _():
            pltpu.make_async_copy(src, dst, t_r.at[slot]).start()

        @pl.when(jnp.logical_not(me))
        def _():
            cp.start()

    sends = []

    def go(cp):
        cp.start()
        sends.append(cp)

    kl = pl.ds(pl.multiple_of(128 * y, 128), 128)
    go(remote(wq, wbuf.at[core, y], y_s.at[0, 0], y_r.at[0, 0], row, yr))
    go(remote(wq, wbuf.at[core, y], y_s.at[1, 0], y_r.at[1, 0], row, yl))
    go(remote(wkv, kvw.at[core, :, kl], yk_s.at[0, 0], yk_r.at[0, 0], row, yr))
    go(remote(wkv, kvw.at[core, :, kl], yk_s.at[1, 0], yk_r.at[1, 0], row, yl))
    go(remote(wq, wbuf.at[core, y], c_s.at[0], c_r.at[0], prow, col))
    go(remote(wkv, kvw.at[core, :, kl], c_s.at[0], c_r.at[1], prow, col))

    def ring_send(buf, ss, rs, s, h):
        hs = pl.ds(HALF * h, HALF)
        a = (z + NZ - s) % NZ
        b = (z + s) % NZ
        if s < 3 or h == 0:
            go(remote(buf.at[a, hs], buf.at[a, hs], ss.at[0, s, h], rs.at[0, s, h], row, zr))
        if s < 3 or h == 1:
            go(remote(buf.at[b, hs], buf.at[b, hs], ss.at[1, s, h], rs.at[1, s, h], row, zl))

    def ring_wait(buf, rs, s, h):
        hs = pl.ds(HALF * h, HALF)
        if s < 3 or h == 0:
            wait_bytes(buf.at[(z + NZ - s - 1) % NZ, hs], rs.at[0, s, h])
        if s < 3 or h == 1:
            wait_bytes(buf.at[(z + s + 1) % NZ, hs], rs.at[1, s, h])

    def ring_step(buf, ss, rs, s, h):
        ring_wait(buf, rs, s, h)
        if s < 3:
            ring_send(buf, ss, rs, s + 1, h)

    for h in range(2):
        wait_bytes(hbuf.at[z, pl.ds(HALF * h, HALF)], t_r.at[h])
        ring_send(hbuf, z_s, z_r, 0, h)

    ring_step(hbuf, z_s, z_r, 0, 0)

    y1, y3, y2 = (y + 1) % NY, (y + 3) % NY, (y + 2) % NY

    def weight_hop(buf, sems, rsems, c_sem, half_rows):
        wait_bytes(buf.at[core, y3], rsems.at[0, 0])
        go(remote(buf.at[core, y3, pl.ds(0, half_rows)], buf.at[core, y3, pl.ds(0, half_rows)],
                  sems.at[0, 1], rsems.at[0, 1], row, yr))
        wait_bytes(buf.at[core, y1], rsems.at[1, 0])
        go(remote(buf.at[core, y1, pl.ds(half_rows, half_rows)], buf.at[core, y1, pl.ds(half_rows, half_rows)],
                  sems.at[1, 1], rsems.at[1, 1], row, yl))
        for b in (y3, y1):
            go(remote(buf.at[core, b], buf.at[core, b], c_s.at[0], c_sem, prow, col))

    def weight_last(buf, rsems, c_sem, half_rows):
        wait_bytes(buf.at[core, y2, pl.ds(0, half_rows)], rsems.at[0, 1])
        wait_bytes(buf.at[core, y2, pl.ds(half_rows, half_rows)], rsems.at[1, 1])
        go(remote(buf.at[core, y2], buf.at[core, y2], c_s.at[0], c_sem, prow, col))

    def lanes(b):
        return pl.ds(pl.multiple_of(128 * b, 128), 128)

    weight_hop(wbuf, y_s, y_r, c_r.at[0], KROWS // 2)
    ring_step(hbuf, z_s, z_r, 1, 0)
    ring_step(hbuf, z_s, z_r, 0, 1)
    l3, l1, l2 = lanes(y3), lanes(y1), lanes(y2)
    top, bot = pl.ds(0, 256), pl.ds(256, 256)
    wait_bytes(kvw.at[core, :, l3], yk_r.at[0, 0])
    go(remote(kvw.at[core, top, l3], kvw.at[core, top, l3], yk_s.at[0, 1], yk_r.at[0, 1], row, yr))
    wait_bytes(kvw.at[core, :, l1], yk_r.at[1, 0])
    go(remote(kvw.at[core, bot, l1], kvw.at[core, bot, l1], yk_s.at[1, 1], yk_r.at[1, 1], row, yl))
    for b in (l3, l1):
        go(remote(kvw.at[core, :, b], kvw.at[core, :, b], c_s.at[0], c_r.at[1], prow, col))

    ring_step(hbuf, z_s, z_r, 2, 0)
    ring_step(hbuf, z_s, z_r, 1, 1)

    weight_last(wbuf, y_r, c_r.at[0], KROWS // 2)
    wait_bytes(kvw.at[core, top, l2], yk_r.at[0, 1])
    wait_bytes(kvw.at[core, bot, l2], yk_r.at[1, 1])
    go(remote(kvw.at[core, :, l2], kvw.at[core, :, l2], c_s.at[0], c_r.at[1], prow, col))

    other = 1 - core
    wait_bytes(wbuf.at[other], c_r.at[0])
    wait_bytes(kvw.at[other], c_r.at[1])
    for c in own:
        c.wait()

    lane512 = lax.broadcasted_iota(jnp.int32, (HALF, 512), 1) % 128 // 64

    def project(zi, h):
        hs = pl.ds(HALF * h, HALF)
        at = pl.multiple_of(2048 * x + COLS * zi, COLS)
        hv = hbuf[zi, hs].astype(F32)
        sq = hv * hv
        ssacc[hs] += sq[:, :128] + sq[:, 128:]
        hg = (hv * gain[:, pl.ds(at, COLS)]).astype(BF)
        kr = pl.ds(pl.multiple_of(zi % 4 * 256, 256), 256)
        for b in range(4):
            acc[b, hs] += jnp.dot(hg, wbuf[zi // 4, b, kr, :], preferred_element_type=F32)
        kk = pl.ds(pl.multiple_of(zi % 2 * 256, 256), 256)
        part = jnp.dot(hg, kvw[zi // 4, kk, :], preferred_element_type=F32)
        kvacc[hs] += jnp.where(lane512 == zi % 4 // 2, part, 0.0)

    k_copies = []

    def reduce_kv(h):
        hs = pl.ds(HALF * h, HALF)
        for dx in range(4):
            xt = (x + dx) % NX
            kvs[dx, hs] = kvacc[hs, lanes(xt)].astype(BF)
            for jq in (2 * h, 2 * h + 1):
                piece = kvs.at[dx, pl.ds(128 * jq, 128)]
                dst = kvrx.at[(4 - dx) % 4 * 4 + (zq + 4 - jq) % 4]
                cp = remote(piece, dst, k_s.at[0], k_r.at[0], 2 * xt + core, 8 * y + 4 * g + jq)
                if dx:
                    go(cp)
                else:
                    me = zq == jq
                    k_copies.append((cp, me))

                    @pl.when(me)
                    def _():
                        pltpu.make_async_copy(piece, dst, k_r.at[0]).start()

                    @pl.when(jnp.logical_not(me))
                    def _():
                        cp.start()

    def reduce_q(h):
        hs = pl.ds(HALF * h, HALF)
        for dx in range(1, 4):
            xt = (x + dx) % NX
            qs[dx - 1, hs] = acc[xt, hs].astype(BF)
            go(remote(qs.at[dx - 1, hs], qrx.at[dx - 1, hs], q_s.at[0], q_r.at[0], 2 * xt + core, col))

    def first_half(i, _):
        project((z + NZ - 3 + i) % NZ, 0)
        return 0

    def second_half(i, _):
        project((z + NZ - 3 + i) % NZ, 1)
        return 0

    lax.fori_loop(0, 3, first_half, 0)
    ring_step(hbuf, z_s, z_r, 3, 0)
    lax.fori_loop(3, 5, first_half, 0)
    ring_step(hbuf, z_s, z_r, 2, 1)
    lax.fori_loop(5, NZ, first_half, 0)
    reduce_kv(0)
    reduce_q(0)
    lax.fori_loop(0, 7, second_half, 0)
    ring_step(hbuf, z_s, z_r, 3, 1)
    project((z + 4) % NZ, 1)
    reduce_kv(1)
    ssb[0] = lax.dot_general(
        jnp.ones((8, 128), F32), ssacc[...], (((1,), (1,)), ((), ())),
        precision=lax.Precision.HIGHEST, preferred_element_type=F32,
    )
    for dx in range(1, 4):
        go(remote(ssb.at[0], ssb.at[dx], ss_s.at[0], ss_r.at[0], 2 * ((x + dx) % NX) + core, col))
    reduce_q(1)

    wait_bytes(ssb.at[pl.ds(1, 3)], ss_r.at[0])
    total = ssb[0] + ssb[1] + ssb[2] + ssb[3]
    r8 = lax.rsqrt(total / D + 1e-05)
    rcol[...] = lax.dot_general(
        r8, jnp.full((8, 128), 0.125, F32), (((0,), (0,)), ((), ())),
        precision=lax.Precision.HIGHEST, preferred_element_type=F32,
    )

    wait_bytes(kvrx, k_r.at[0])
    mine = pl.ds(pl.multiple_of(128 * zq, 128), 128)
    lane = lax.broadcasted_iota(jnp.int32, (128, 128), 1) // 32
    keys = jnp.zeros((128, 128), F32)
    vals = jnp.zeros((128, 128), F32)
    for j in range(4):
        dj = (j + 4 - zq) % 4
        part = kvrx[dj].astype(F32)
        for dx in range(1, 4):
            part += kvrx[4 * dx + dj].astype(F32)
        part = part + pltpu.roll(part, 64, 1)
        keys = jnp.where(lane == j, part if j % 2 == 0 else pltpu.roll(part, 32, 1), keys)
        vals = jnp.where(lane == j, part if j % 2 == 1 else pltpu.roll(part, 96, 1), vals)
    keys = keys * rcol[mine, :]
    vals = vals * rcol[mine, :]
    keys = keys * ctab[mine, :] + pltpu.roll(keys, 64, 1) * stab[mine, :]

    def block_at(yy, jj):
        dd = 2 * yy + core
        return jnp.where(jj < 2, 2 * dd, 2 * (15 - dd)) + jj % 2

    here = block_at(y, zq)
    kvb[here, :, 0:128] = keys.astype(BF)
    kvb[here, :, 128:256] = vals.astype(BF)
    kv_here = [block_at(y, (zq + dj) % 4) for dj in range(4)]
    kv_left = [block_at(y3, (zq + dj) % 4) for dj in range(4)]
    kv_right = [block_at(y1, (zq + dj) % 4) for dj in range(4)]
    kv_far = [block_at(y2, (zq + dj) % 4) for dj in range(4)]
    half0, half1 = pl.ds(0, 64), pl.ds(64, 64)

    def to_partner(b):
        go(remote(kvb.at[b], kvb.at[b], p_s.at[0], p_r.at[0], prow, col))

    def kv_hop(dj):
        b = kv_here[dj]
        go(remote(kvb.at[b], kvb.at[b], b_s.at[0], bl_r.at[dj], row, yr))
        go(remote(kvb.at[b], kvb.at[b], b_s.at[0], br_r.at[dj], row, yl))
        to_partner(b)

    for dj in (1, 3, 2):
        go(remote(kvb.at[here], kvb.at[here], b_s.at[0], b_r.at[4 - dj], row, 8 * y + 4 * g + (zq + dj) % 4))
    kv_hop(0)
    for dj in (1, 3, 2):
        wait_bytes(kvb.at[kv_here[dj]], b_r.at[dj])
        kv_hop(dj)
    for dj in (0, 1, 3, 2):
        left, right = kv_left[dj], kv_right[dj]
        wait_bytes(kvb.at[left], bl_r.at[dj])
        go(remote(kvb.at[left, half0], kvb.at[left, half0], b_s.at[0], bf_r.at[0, dj], row, yr))
        wait_bytes(kvb.at[right], br_r.at[dj])
        go(remote(kvb.at[right, half1], kvb.at[right, half1], b_s.at[0], bf_r.at[1, dj], row, yl))
        to_partner(left)
        to_partner(right)

    wait_bytes(qrx, q_r.at[0])
    for h in range(2):
        hl = slice(128 * h, 128 * h + 128)
        q = acc[x, :, hl]
        for i in range(3):
            q += qrx[i, :, hl].astype(F32)
        q = q * rcol[...]
        q = (q * ctab[...] + pltpu.roll(q, 64, 1) * stab[...]).astype(BF)
        for k in range(2):
            qb[k, HALF * h : HALF * (h + 1), :] = q[HALF * k : HALF * (k + 1), :]


    for dj in (0, 1, 3, 2):
        far = kv_far[dj]
        wait_bytes(kvb.at[far, half0], bf_r.at[0, dj])
        wait_bytes(kvb.at[far, half1], bf_r.at[1, dj])
        to_partner(far)
    wait_bytes(kvb.at[pl.ds(0, 16)], p_r.at[0])

    go(remote(wo, wob.at[core, y], yo_s.at[0, 0], yo_r.at[0, 0], row, yr))
    go(remote(wo, wob.at[core, y], yo_s.at[1, 0], yo_r.at[1, 0], row, yl))
    go(remote(wo, wob.at[core, y], c_s.at[0], c_r.at[2], prow, col))

    rows = 2 * HALF
    tri = (
        lax.broadcasted_iota(jnp.int32, (rows, HALF), 0) % HALF
        >= lax.broadcasted_iota(jnp.int32, (rows, HALF), 1)
    )

    for k in range(2):
        qk = qb[k]

        def scores(t):
            key = kvb[pl.ds(2 * t, 2), :, 0:128].reshape(HALF, 128)
            val = kvb[pl.ds(2 * t, 2), :, 128:256].reshape(HALF, 128)
            s = lax.dot_general(qk, key, (((1,), (1,)), ((), ())), preferred_element_type=F32)
            return s * EXP2_SCALE, val

        last = d if k == 0 else 15 - d
        s, val = scores(last)
        s = jnp.where(tri, s, -jnp.inf)
        top_ = jnp.max(s, axis=1, keepdims=True)
        p = jnp.exp2(s - top_)
        den = jnp.sum(p, axis=1, keepdims=True)
        num = jnp.dot(p.astype(BF), val, preferred_element_type=F32)

        def step(t, carry):
            top_, den, num = carry
            s, val = scores(t)
            new = jnp.maximum(top_, jnp.max(s, axis=1, keepdims=True))
            fix = jnp.exp2(top_ - new)
            p = jnp.exp2(s - new)
            den = den * fix + jnp.sum(p, axis=1, keepdims=True)
            num = num * fix + jnp.dot(p.astype(BF), val, preferred_element_type=F32)
            return new, den, num

        top_, den, num = lax.fori_loop(0, last, step, (top_, den, num))
        res = (num / den).astype(BF)
        for h in range(2):
            hb[z, HALF * k : HALF * (k + 1), 128 * h : 128 * (h + 1)] = res[HALF * h : HALF * (h + 1), :]
        ring_send(hb, g_s, g_r, 0, k)

    ring_step(hb, g_s, g_r, 0, 0)
    weight_hop(wob, yo_s, yo_r, c_r.at[2], KROWS // 2)
    ring_step(hb, g_s, g_r, 1, 0)
    ring_step(hb, g_s, g_r, 0, 1)
    ring_step(hb, g_s, g_r, 2, 0)
    ring_step(hb, g_s, g_r, 1, 1)
    weight_last(wob, yo_r, c_r.at[2], KROWS // 2)
    wait_bytes(wob.at[other], c_r.at[2])
    acc[...] = jnp.zeros_like(acc)

    def finish(zi, h):
        hs = pl.ds(HALF * h, HALF)
        hg = hb[zi, hs]
        kr = pl.ds(pl.multiple_of(zi % 4 * 256, 256), 256)
        for b in range(4):
            acc[b, hs] += jnp.dot(hg, wob[zi // 4, b, kr, :], preferred_element_type=F32)

    def first_out(i, _):
        finish((z + NZ - 3 + i) % NZ, 0)
        return 0

    def second_out(i, _):
        finish((z + NZ - 3 + i) % NZ, 1)
        return 0

    def reduce_out(h):
        hs = pl.ds(HALF * h, HALF)
        for dx in range(1, 4):
            xt = (x + dx) % NX
            osb[dx - 1, hs] = acc[xt, hs].astype(BF)
            go(remote(osb.at[dx - 1, hs], orx.at[dx - 1, hs], o_s.at[h], o_r.at[h], 2 * xt + core, col))

    o_copies = []

    def deliver(h):
        hs = pl.ds(HALF * h, HALF)
        wait_bytes(orx.at[:, hs], o_r.at[h])
        v = acc[x, hs]
        for i in range(3):
            v += orx[i, hs].astype(F32)
        fin[h] = v.astype(BF)
        tr = y if h == 0 else 7 - y
        ha = core if h == 0 else 1 - core
        me = jnp.logical_and(tr == row, x == y)
        src, dst, rs = fin.at[h], frx.at[ha], f_r.at[ha]
        cp = remote(src, dst, f_s.at[h], rs, tr, 8 * x + z)
        o_copies.append((cp, me))

        @pl.when(me)
        def _():
            pltpu.make_async_copy(src, dst, rs).start()

        @pl.when(jnp.logical_not(me))
        def _():
            cp.start()

    lax.fori_loop(0, 3, first_out, 0)
    ring_step(hb, g_s, g_r, 3, 0)
    lax.fori_loop(3, 5, first_out, 0)
    ring_step(hb, g_s, g_r, 2, 1)
    lax.fori_loop(5, NZ, first_out, 0)
    reduce_out(0)
    lax.fori_loop(0, 7, second_out, 0)
    ring_step(hb, g_s, g_r, 3, 1)
    finish((z + 4) % NZ, 1)
    reduce_out(1)
    deliver(0)
    deliver(1)
    for ha in range(2):
        wait_bytes(frx.at[ha], f_r.at[ha])
        out[HALF * ha : HALF * (ha + 1), :] = frx[ha]

    for cp in sends:
        cp.wait_send()
    for cp, me in t_copies + k_copies + o_copies:

        @pl.when(jnp.logical_not(me))
        def _():
            cp.wait_send()


def per_device(hidden, norm_gain, wq, wk, wv, wo):
    row, col = lax.axis_index("row"), lax.axis_index("col")
    d = 2 * (col // NZ) + row % 2
    i = jnp.arange(TOK)
    positions = jnp.where(i < HALF, HALF * d + i, HALF * (15 - d) + i - HALF)
    steps = jnp.arange(HD // 2).astype(F32)
    freqs = 10000.0 ** (-steps / (HD // 2))
    angles = positions.astype(F32)[:, None] * freqs[None, :]
    cosine, sine = jnp.cos(angles), jnp.sin(angles)
    ctab = jnp.concatenate([cosine, cosine], axis=1)
    stab = jnp.concatenate([-sine, sine], axis=1)
    both = jnp.concatenate([wk, wv], axis=1)
    wkv = jnp.concatenate([both[:512], both[512:]], axis=1)
    dma = pltpu.SemaphoreType.DMA
    vmem = pl.BlockSpec(memory_space=pltpu.VMEM)
    anyw = pl.BlockSpec(memory_space=pl.ANY)
    scratch = [
        pltpu.VMEM((NZ, TOK, COLS), BF),
        pltpu.VMEM((2, NY, KROWS, COLS), BF),
        pltpu.VMEM((2, 512, 512), BF),
        pltpu.VMEM((2, NY, KROWS, COLS), BF),
        pltpu.VMEM((NY, TOK, COLS), F32),
        pltpu.VMEM((TOK, 512), F32),
        pltpu.VMEM((TOK, 128), F32),
        pltpu.VMEM((3, TOK, COLS), BF),
        pltpu.VMEM((3, TOK, COLS), BF),
        pltpu.VMEM((4, TOK, 128), BF),
        pltpu.VMEM((16, 128, 128), BF),
        pltpu.VMEM((32, 128, 256), BF),
        pltpu.VMEM((4, 8, TOK), F32),
        pltpu.VMEM((TOK, 128), F32),
        pltpu.VMEM((2, TOK, 128), BF),
        pltpu.VMEM((NZ, TOK, COLS), BF),
        pltpu.VMEM((3, TOK, COLS), BF),
        pltpu.VMEM((3, TOK, COLS), BF),
        pltpu.VMEM((2, HALF, COLS), BF),
        pltpu.VMEM((2, HALF, COLS), BF),
        dma((2,)), dma((2,)),
        dma((2, 4, 2)), dma((2, 4, 2)),
        dma((2, 4, 2)), dma((2, 4, 2)),
        dma((2, 2)), dma((2, 2)),
        dma((2, 2)), dma((2, 2)),
        dma((2, 2)), dma((2, 2)),
        dma((1,)), dma((3,)),
        dma((3,)),
        dma((1,)), dma((1,)),
        dma((1,)), dma((1,)),
        dma((1,)), dma((1,)),
        dma((1,)), dma((4,)), dma((4,)), dma((4,)), dma((2, 4)),
        dma((1,)), dma((1,)),
        dma((2,)), dma((2,)),
        dma((2,)), dma((2,)),
    ]
    return pl.pallas_call(
        kernel,
        out_shape=jax.ShapeDtypeStruct((TOK, COLS), BF),
        in_specs=[anyw, vmem, anyw, anyw, anyw, vmem, vmem],
        out_specs=vmem,
        scratch_shapes=scratch,
        compiler_params=pltpu.CompilerParams(
            collective_id=0, has_side_effects=True, vmem_limit_bytes=56 * 1024 * 1024
        ),
    )(hidden, norm_gain.reshape(1, D), wq, wkv, wo, ctab, stab)


def solution(mesh):
    spec = P("row", "col")
    return jax.shard_map(
        per_device, mesh=mesh, in_specs=(spec, P(), spec, spec, spec, spec), out_specs=spec, check_vma=False
    )
```

```python
import functools

import jax
import jax.numpy as jnp
from jax import lax
from jax.experimental import pallas as pl
from jax.experimental.pallas import tpu as pltpu
from jax.sharding import PartitionSpec as P

MESH = pl.DeviceIdType.MESH
BF = jnp.bfloat16
F32 = jnp.float32
HD = 128
TOK = 512
HALF = 256
COLS = 256
KROWS = 1024
NX, NY, NZ = 4, 4, 8
D = 8192
EXP2_SCALE = HD ** (-0.5) * 1.4426950408889634


def wait_bytes(ref, sem):
    pltpu.make_async_copy(ref, ref, sem).wait()


def kernel(
    hid, gain, freq, wq, wkv, wo, out,
    ctab, stab, hbuf, wbuf, kvw, wob, acc, kvacc, ssacc, qs, qrx, kvs, kvrx, kvb, ssb, rcol, qb, hb, osb, orx, fin, frx,
    t_s, t_r, z_s, z_r, g_s, g_r, y_s, y_r, yk_s, yk_r, yo_s, yo_r,
    c_s, c_r, loc, q_s, q_r, ss_s, ss_r, k_s, k_r, b_s, b_r, bl_r, br_r, bf_r, p_s, p_r, o_s, o_r, f_s, f_r,
):
    row = lax.axis_index("row")
    col = lax.axis_index("col")
    x, core = row // 2, row % 2
    y, z = col // NZ, col % NZ
    g, zq = z // 4, z % 4
    d = 2 * y + core
    prow = row + 1 - 2 * core

    def remote(src, dst, ss, rs, r, c):
        return pltpu.make_async_remote_copy(
            src_ref=src, dst_ref=dst, send_sem=ss, recv_sem=rs, device_id=(r, c), device_id_type=MESH
        )

    zr, zl = 8 * y + (z + 1) % NZ, 8 * y + (z + NZ - 1) % NZ
    yr, yl = 8 * ((y + 1) % NY) + z, 8 * ((y + NY - 1) % NY) + z
    low = row < 4
    t_y = jnp.where(low, row, 7 - row)

    barrier = pltpu.get_barrier_semaphore()

    def greet(r, c):
        pl.semaphore_signal(barrier, inc=1, device_id=(r, c), device_id_type=MESH)

    def greet_maybe_self(r, c):
        me = jnp.logical_and(r == row, c == col)

        @pl.when(jnp.logical_not(me))
        def _():
            greet(r, c)

        return jnp.where(me, 0, 1)

    count = 0
    for c in (zr, zl, yr, yl):
        greet(row, c)
        count += 1
    greet(prow, col)
    count += 1
    count += greet_maybe_self(y, 8 * x + z)
    count += greet_maybe_self(7 - y, 8 * x + z)
    for dx in range(4):
        for dj in range(4):
            if dx or dj:
                greet(2 * ((x + dx) % NX) + core, 8 * y + 4 * g + (zq + dj) % 4)
                count += 1
    for cs in range(2):
        count += greet_maybe_self(2 * y + cs, 8 * t_y + z)

    own = [
        pltpu.make_async_copy(wq, wbuf.at[core, y], loc.at[0]),
        pltpu.make_async_copy(wkv, kvw.at[core, :, pl.ds(pl.multiple_of(128 * y, 128), 128)], loc.at[1]),
        pltpu.make_async_copy(wo, wob.at[core, y], loc.at[2]),
    ]
    for c in own:
        c.start()
    acc[...] = jnp.zeros_like(acc)
    kvacc[...] = jnp.zeros_like(kvacc)
    ssacc[...] = jnp.zeros_like(ssacc)
    pl.semaphore_wait(barrier, count)

    t_copies = []
    for h in range(2):
        tcore = jnp.where(low, h, 1 - h)
        slot = jnp.where(low, 0, 1)
        tr, tc = 2 * y + tcore, 8 * t_y + z
        me = jnp.logical_and(tr == row, tc == col)
        src = hid.at[pl.ds(HALF * h, HALF)]
        dst = hbuf.at[z, pl.ds(pl.multiple_of(HALF * slot, HALF), HALF)]
        cp = remote(src, dst, t_s.at[h], t_r.at[slot], tr, tc)
        t_copies.append((cp, me))

        @pl.when(me)
        def _():
            pltpu.make_async_copy(src, dst, t_r.at[slot]).start()

        @pl.when(jnp.logical_not(me))
        def _():
            cp.start()

    sends = []

    def go(cp):
        cp.start()
        sends.append(cp)

    kl = pl.ds(pl.multiple_of(128 * y, 128), 128)
    go(remote(wq, wbuf.at[core, y], y_s.at[0, 0], y_r.at[0, 0], row, yr))
    go(remote(wq, wbuf.at[core, y], y_s.at[1, 0], y_r.at[1, 0], row, yl))
    go(remote(wkv, kvw.at[core, :, kl], yk_s.at[0, 0], yk_r.at[0, 0], row, yr))
    go(remote(wkv, kvw.at[core, :, kl], yk_s.at[1, 0], yk_r.at[1, 0], row, yl))
    go(remote(wq, wbuf.at[core, y], c_s.at[0], c_r.at[0], prow, col))
    go(remote(wkv, kvw.at[core, :, kl], c_s.at[0], c_r.at[1], prow, col))

    def ring_send(buf, ss, rs, s, h):
        hs = pl.ds(HALF * h, HALF)
        a = (z + NZ - s) % NZ
        b = (z + s) % NZ
        if s < 3 or h == 0:
            go(remote(buf.at[a, hs], buf.at[a, hs], ss.at[0, s, h], rs.at[0, s, h], row, zr))
        if s < 3 or h == 1:
            go(remote(buf.at[b, hs], buf.at[b, hs], ss.at[1, s, h], rs.at[1, s, h], row, zl))

    def ring_wait(buf, rs, s, h):
        hs = pl.ds(HALF * h, HALF)
        if s < 3 or h == 0:
            wait_bytes(buf.at[(z + NZ - s - 1) % NZ, hs], rs.at[0, s, h])
        if s < 3 or h == 1:
            wait_bytes(buf.at[(z + s + 1) % NZ, hs], rs.at[1, s, h])

    def ring_step(buf, ss, rs, s, h):
        ring_wait(buf, rs, s, h)
        if s < 3:
            ring_send(buf, ss, rs, s + 1, h)

    for h in range(2):
        wait_bytes(hbuf.at[z, pl.ds(HALF * h, HALF)], t_r.at[h])
        ring_send(hbuf, z_s, z_r, 0, h)

    spot = lax.broadcasted_iota(jnp.int32, (TOK, HD), 0)
    spot = jnp.where(spot < HALF, HALF * d + spot, HALF * (14 - d) + spot)
    angle = spot.astype(F32) * freq[...]
    ctab[...] = jnp.cos(angle)
    sine = jnp.sin(angle)
    stab[...] = jnp.where(lax.broadcasted_iota(jnp.int32, (TOK, HD), 1) < HD // 2, -sine, sine)

    ring_step(hbuf, z_s, z_r, 0, 0)

    y1, y3, y2 = (y + 1) % NY, (y + 3) % NY, (y + 2) % NY

    def weight_hop(buf, sems, rsems, c_sem, half_rows):
        wait_bytes(buf.at[core, y3], rsems.at[0, 0])
        go(remote(buf.at[core, y3, pl.ds(0, half_rows)], buf.at[core, y3, pl.ds(0, half_rows)],
                  sems.at[0, 1], rsems.at[0, 1], row, yr))
        wait_bytes(buf.at[core, y1], rsems.at[1, 0])
        go(remote(buf.at[core, y1, pl.ds(half_rows, half_rows)], buf.at[core, y1, pl.ds(half_rows, half_rows)],
                  sems.at[1, 1], rsems.at[1, 1], row, yl))
        for b in (y3, y1):
            go(remote(buf.at[core, b], buf.at[core, b], c_s.at[0], c_sem, prow, col))

    def weight_last(buf, rsems, c_sem, half_rows):
        wait_bytes(buf.at[core, y2, pl.ds(0, half_rows)], rsems.at[0, 1])
        wait_bytes(buf.at[core, y2, pl.ds(half_rows, half_rows)], rsems.at[1, 1])
        go(remote(buf.at[core, y2], buf.at[core, y2], c_s.at[0], c_sem, prow, col))

    def lanes(b):
        return pl.ds(pl.multiple_of(128 * b, 128), 128)

    weight_hop(wbuf, y_s, y_r, c_r.at[0], KROWS // 2)
    ring_step(hbuf, z_s, z_r, 1, 0)
    ring_step(hbuf, z_s, z_r, 0, 1)
    l3, l1, l2 = lanes(y3), lanes(y1), lanes(y2)
    top, bot = pl.ds(0, 256), pl.ds(256, 256)
    wait_bytes(kvw.at[core, :, l3], yk_r.at[0, 0])
    go(remote(kvw.at[core, top, l3], kvw.at[core, top, l3], yk_s.at[0, 1], yk_r.at[0, 1], row, yr))
    wait_bytes(kvw.at[core, :, l1], yk_r.at[1, 0])
    go(remote(kvw.at[core, bot, l1], kvw.at[core, bot, l1], yk_s.at[1, 1], yk_r.at[1, 1], row, yl))
    for b in (l3, l1):
        go(remote(kvw.at[core, :, b], kvw.at[core, :, b], c_s.at[0], c_r.at[1], prow, col))

    ring_step(hbuf, z_s, z_r, 2, 0)
    ring_step(hbuf, z_s, z_r, 1, 1)

    weight_last(wbuf, y_r, c_r.at[0], KROWS // 2)
    wait_bytes(kvw.at[core, top, l2], yk_r.at[0, 1])
    wait_bytes(kvw.at[core, bot, l2], yk_r.at[1, 1])
    go(remote(kvw.at[core, :, l2], kvw.at[core, :, l2], c_s.at[0], c_r.at[1], prow, col))

    other = 1 - core
    wait_bytes(wbuf.at[other], c_r.at[0])
    wait_bytes(kvw.at[other], c_r.at[1])
    for c in own:
        c.wait()

    lane512 = lax.broadcasted_iota(jnp.int32, (HALF, 512), 1) % 128 // 64

    def project(zi, h):
        hs = pl.ds(HALF * h, HALF)
        at = pl.multiple_of(2048 * x + COLS * zi, COLS)
        hv = hbuf[zi, hs].astype(F32)
        sq = hv * hv
        ssacc[hs] += sq[:, :128] + sq[:, 128:]
        hg = (hv * gain[:, pl.ds(at, COLS)]).astype(BF)
        kr = pl.ds(pl.multiple_of(zi % 4 * 256, 256), 256)
        for b in range(4):
            acc[b, hs] += jnp.dot(hg, wbuf[zi // 4, b, kr, :], preferred_element_type=F32)
        kk = pl.ds(pl.multiple_of(zi % 2 * 256, 256), 256)
        part = jnp.dot(hg, kvw[zi // 4, kk, :], preferred_element_type=F32)
        kvacc[hs] += jnp.where(lane512 == zi % 4 // 2, part, 0.0)

    k_copies = []

    def reduce_kv(h):
        hs = pl.ds(HALF * h, HALF)
        for dx in range(4):
            xt = (x + dx) % NX
            kvs[dx, hs] = kvacc[hs, lanes(xt)].astype(BF)
            for jq in (2 * h, 2 * h + 1):
                piece = kvs.at[dx, pl.ds(128 * jq, 128)]
                dst = kvrx.at[(4 - dx) % 4 * 4 + (zq + 4 - jq) % 4]
                cp = remote(piece, dst, k_s.at[0], k_r.at[0], 2 * xt + core, 8 * y + 4 * g + jq)
                if dx:
                    go(cp)
                else:
                    me = zq == jq
                    k_copies.append((cp, me))

                    @pl.when(me)
                    def _():
                        pltpu.make_async_copy(piece, dst, k_r.at[0]).start()

                    @pl.when(jnp.logical_not(me))
                    def _():
                        cp.start()

    def reduce_q(h):
        hs = pl.ds(HALF * h, HALF)
        for dx in range(1, 4):
            xt = (x + dx) % NX
            qs[dx - 1, hs] = acc[xt, hs].astype(BF)
            go(remote(qs.at[dx - 1, hs], qrx.at[dx - 1, hs], q_s.at[0], q_r.at[0], 2 * xt + core, col))

    def first_half(i, _):
        project((z + NZ - 3 + i) % NZ, 0)
        return 0

    def second_half(i, _):
        project((z + NZ - 3 + i) % NZ, 1)
        return 0

    lax.fori_loop(0, 3, first_half, 0)
    ring_step(hbuf, z_s, z_r, 3, 0)
    lax.fori_loop(3, 5, first_half, 0)
    ring_step(hbuf, z_s, z_r, 2, 1)
    lax.fori_loop(5, NZ, first_half, 0)
    reduce_kv(0)
    reduce_q(0)
    lax.fori_loop(0, 7, second_half, 0)
    ring_step(hbuf, z_s, z_r, 3, 1)
    project((z + 4) % NZ, 1)
    reduce_kv(1)
    ssb[0] = lax.dot_general(
        jnp.ones((8, 128), F32), ssacc[...], (((1,), (1,)), ((), ())),
        precision=lax.Precision.HIGHEST, preferred_element_type=F32,
    )
    for dx in range(1, 4):
        go(remote(ssb.at[0], ssb.at[dx], ss_s.at[0], ss_r.at[0], 2 * ((x + dx) % NX) + core, col))
    reduce_q(1)

    wait_bytes(ssb.at[pl.ds(1, 3)], ss_r.at[0])
    total = ssb[0] + ssb[1] + ssb[2] + ssb[3]
    r8 = lax.rsqrt(total / D + 1e-05)
    rcol[...] = lax.dot_general(
        r8, jnp.full((8, 128), 0.125, F32), (((0,), (0,)), ((), ())),
        precision=lax.Precision.HIGHEST, preferred_element_type=F32,
    )

    wait_bytes(kvrx, k_r.at[0])
    mine = pl.ds(pl.multiple_of(128 * zq, 128), 128)
    lane = lax.broadcasted_iota(jnp.int32, (128, 128), 1) // 32
    keys = jnp.zeros((128, 128), F32)
    vals = jnp.zeros((128, 128), F32)
    for j in range(4):
        dj = (j + 4 - zq) % 4
        part = kvrx[dj].astype(F32)
        for dx in range(1, 4):
            part += kvrx[4 * dx + dj].astype(F32)
        part = part + pltpu.roll(part, 64, 1)
        keys = jnp.where(lane == j, part if j % 2 == 0 else pltpu.roll(part, 32, 1), keys)
        vals = jnp.where(lane == j, part if j % 2 == 1 else pltpu.roll(part, 96, 1), vals)
    keys = keys * rcol[mine, :]
    vals = vals * rcol[mine, :]
    keys = keys * ctab[mine, :] + pltpu.roll(keys, 64, 1) * stab[mine, :]

    def block_at(yy, jj):
        dd = 2 * yy + core
        return jnp.where(jj < 2, 2 * dd, 2 * (15 - dd)) + jj % 2

    here = block_at(y, zq)
    kvb[here, :, 0:128] = keys.astype(BF)
    kvb[here, :, 128:256] = vals.astype(BF)
    kv_here = [block_at(y, (zq + dj) % 4) for dj in range(4)]
    kv_left = [block_at(y3, (zq + dj) % 4) for dj in range(4)]
    kv_right = [block_at(y1, (zq + dj) % 4) for dj in range(4)]
    kv_far = [block_at(y2, (zq + dj) % 4) for dj in range(4)]
    half0, half1 = pl.ds(0, 64), pl.ds(64, 64)

    def to_partner(b):
        go(remote(kvb.at[b], kvb.at[b], p_s.at[0], p_r.at[0], prow, col))

    def kv_hop(dj):
        b = kv_here[dj]
        go(remote(kvb.at[b], kvb.at[b], b_s.at[0], bl_r.at[dj], row, yr))
        go(remote(kvb.at[b], kvb.at[b], b_s.at[0], br_r.at[dj], row, yl))
        to_partner(b)

    for dj in (1, 3, 2):
        go(remote(kvb.at[here], kvb.at[here], b_s.at[0], b_r.at[4 - dj], row, 8 * y + 4 * g + (zq + dj) % 4))
    kv_hop(0)
    for dj in (1, 3, 2):
        wait_bytes(kvb.at[kv_here[dj]], b_r.at[dj])
        kv_hop(dj)
    for dj in (0, 1, 3, 2):
        left, right = kv_left[dj], kv_right[dj]
        wait_bytes(kvb.at[left], bl_r.at[dj])
        go(remote(kvb.at[left, half0], kvb.at[left, half0], b_s.at[0], bf_r.at[0, dj], row, yr))
        wait_bytes(kvb.at[right], br_r.at[dj])
        go(remote(kvb.at[right, half1], kvb.at[right, half1], b_s.at[0], bf_r.at[1, dj], row, yl))
        to_partner(left)
        to_partner(right)

    wait_bytes(qrx, q_r.at[0])
    for h in range(2):
        hl = slice(128 * h, 128 * h + 128)
        q = acc[x, :, hl]
        for i in range(3):
            q += qrx[i, :, hl].astype(F32)
        q = q * rcol[...]
        q = (q * ctab[...] + pltpu.roll(q, 64, 1) * stab[...]).astype(BF)
        for k in range(2):
            qb[k, HALF * h : HALF * (h + 1), :] = q[HALF * k : HALF * (k + 1), :]


    for dj in (0, 1, 3, 2):
        far = kv_far[dj]
        wait_bytes(kvb.at[far, half0], bf_r.at[0, dj])
        wait_bytes(kvb.at[far, half1], bf_r.at[1, dj])
        to_partner(far)
    wait_bytes(kvb.at[pl.ds(0, 16)], p_r.at[0])

    go(remote(wo, wob.at[core, y], yo_s.at[0, 0], yo_r.at[0, 0], row, yr))
    go(remote(wo, wob.at[core, y], yo_s.at[1, 0], yo_r.at[1, 0], row, yl))
    go(remote(wo, wob.at[core, y], c_s.at[0], c_r.at[2], prow, col))

    rows = 2 * HALF
    tri = (
        lax.broadcasted_iota(jnp.int32, (rows, HALF), 0) % HALF
        >= lax.broadcasted_iota(jnp.int32, (rows, HALF), 1)
    )

    for k in range(2):
        qk = qb[k]

        def scores(t):
            key = kvb[pl.ds(2 * t, 2), :, 0:128].reshape(HALF, 128)
            val = kvb[pl.ds(2 * t, 2), :, 128:256].reshape(HALF, 128)
            s = lax.dot_general(qk, key, (((1,), (1,)), ((), ())), preferred_element_type=F32)
            return s * EXP2_SCALE, val

        last = d if k == 0 else 15 - d
        s, val = scores(last)
        s = jnp.where(tri, s, -jnp.inf)
        top_ = jnp.max(s, axis=1, keepdims=True)
        p = jnp.exp2(s - top_)
        den = jnp.sum(p, axis=1, keepdims=True)
        num = jnp.dot(p.astype(BF), val, preferred_element_type=F32)

        def step(t, carry):
            top_, den, num = carry
            s, val = scores(t)
            new = jnp.maximum(top_, jnp.max(s, axis=1, keepdims=True))
            fix = jnp.exp2(top_ - new)
            p = jnp.exp2(s - new)
            den = den * fix + jnp.sum(p, axis=1, keepdims=True)
            num = num * fix + jnp.dot(p.astype(BF), val, preferred_element_type=F32)
            return new, den, num

        top_, den, num = lax.fori_loop(0, last, step, (top_, den, num))
        res = (num / den).astype(BF)
        for h in range(2):
            hb[z, HALF * k : HALF * (k + 1), 128 * h : 128 * (h + 1)] = res[HALF * h : HALF * (h + 1), :]
        ring_send(hb, g_s, g_r, 0, k)

    acc[...] = jnp.zeros_like(acc)
    ring_step(hb, g_s, g_r, 0, 0)
    weight_hop(wob, yo_s, yo_r, c_r.at[2], KROWS // 2)
    ring_step(hb, g_s, g_r, 1, 0)
    ring_step(hb, g_s, g_r, 0, 1)
    ring_step(hb, g_s, g_r, 2, 0)
    ring_step(hb, g_s, g_r, 1, 1)
    weight_last(wob, yo_r, c_r.at[2], KROWS // 2)
    wait_bytes(wob.at[other], c_r.at[2])

    def finish(zi, h):
        hs = pl.ds(HALF * h, HALF)
        hg = hb[zi, hs]
        kr = pl.ds(pl.multiple_of(zi % 4 * 256, 256), 256)
        for b in range(4):
            acc[b, hs] += jnp.dot(hg, wob[zi // 4, b, kr, :], preferred_element_type=F32)

    def first_out(i, _):
        finish((z + NZ - 3 + i) % NZ, 0)
        return 0

    def second_out(i, _):
        finish((z + NZ - 3 + i) % NZ, 1)
        return 0

    def reduce_out(h):
        hs = pl.ds(HALF * h, HALF)
        for dx in range(1, 4):
            xt = (x + dx) % NX
            osb[dx - 1, hs] = acc[xt, hs].astype(BF)
            go(remote(osb.at[dx - 1, hs], orx.at[dx - 1, hs], o_s.at[h], o_r.at[h], 2 * xt + core, col))

    o_copies = []

    def deliver(h):
        hs = pl.ds(HALF * h, HALF)
        wait_bytes(orx.at[:, hs], o_r.at[h])
        v = acc[x, hs]
        for i in range(3):
            v += orx[i, hs].astype(F32)
        fin[h] = v.astype(BF)
        tr = y if h == 0 else 7 - y
        ha = core if h == 0 else 1 - core
        me = jnp.logical_and(tr == row, x == y)
        src, dst, rs = fin.at[h], frx.at[ha], f_r.at[ha]
        cp = remote(src, dst, f_s.at[h], rs, tr, 8 * x + z)
        o_copies.append((cp, me))

        @pl.when(me)
        def _():
            pltpu.make_async_copy(src, dst, rs).start()

        @pl.when(jnp.logical_not(me))
        def _():
            cp.start()

    lax.fori_loop(0, 3, first_out, 0)
    ring_step(hb, g_s, g_r, 3, 0)
    lax.fori_loop(3, 5, first_out, 0)
    ring_step(hb, g_s, g_r, 2, 1)
    lax.fori_loop(5, NZ, first_out, 0)
    reduce_out(0)
    lax.fori_loop(0, 7, second_out, 0)
    ring_step(hb, g_s, g_r, 3, 1)
    finish((z + 4) % NZ, 1)
    reduce_out(1)
    deliver(0)
    deliver(1)
    for ha in range(2):
        wait_bytes(frx.at[ha], f_r.at[ha])
        out[HALF * ha : HALF * (ha + 1), :] = frx[ha]

    for cp in sends:
        cp.wait_send()
    for cp, me in t_copies + k_copies + o_copies:

        @pl.when(jnp.logical_not(me))
        def _():
            cp.wait_send()


def per_device(hidden, norm_gain, wq, wk, wv, wo):
    steps = jnp.arange(HD // 2).astype(F32)
    freqs = 10000.0 ** (-steps / (HD // 2))
    freq = jnp.concatenate([freqs, freqs]).reshape(1, HD)
    both = jnp.concatenate([wk, wv], axis=1)
    wkv = jnp.concatenate([both[:512], both[512:]], axis=1)
    dma = pltpu.SemaphoreType.DMA
    vmem = pl.BlockSpec(memory_space=pltpu.VMEM)
    anyw = pl.BlockSpec(memory_space=pl.ANY)
    scratch = [
        pltpu.VMEM((TOK, HD), F32),
        pltpu.VMEM((TOK, HD), F32),
        pltpu.VMEM((NZ, TOK, COLS), BF),
        pltpu.VMEM((2, NY, KROWS, COLS), BF),
        pltpu.VMEM((2, 512, 512), BF),
        pltpu.VMEM((2, NY, KROWS, COLS), BF),
        pltpu.VMEM((NY, TOK, COLS), F32),
        pltpu.VMEM((TOK, 512), F32),
        pltpu.VMEM((TOK, 128), F32),
        pltpu.VMEM((3, TOK, COLS), BF),
        pltpu.VMEM((3, TOK, COLS), BF),
        pltpu.VMEM((4, TOK, 128), BF),
        pltpu.VMEM((16, 128, 128), BF),
        pltpu.VMEM((32, 128, 256), BF),
        pltpu.VMEM((4, 8, TOK), F32),
        pltpu.VMEM((TOK, 128), F32),
        pltpu.VMEM((2, TOK, 128), BF),
        pltpu.VMEM((NZ, TOK, COLS), BF),
        pltpu.VMEM((3, TOK, COLS), BF),
        pltpu.VMEM((3, TOK, COLS), BF),
        pltpu.VMEM((2, HALF, COLS), BF),
        pltpu.VMEM((2, HALF, COLS), BF),
        dma((2,)), dma((2,)),
        dma((2, 4, 2)), dma((2, 4, 2)),
        dma((2, 4, 2)), dma((2, 4, 2)),
        dma((2, 2)), dma((2, 2)),
        dma((2, 2)), dma((2, 2)),
        dma((2, 2)), dma((2, 2)),
        dma((1,)), dma((3,)),
        dma((3,)),
        dma((1,)), dma((1,)),
        dma((1,)), dma((1,)),
        dma((1,)), dma((1,)),
        dma((1,)), dma((4,)), dma((4,)), dma((4,)), dma((2, 4)),
        dma((1,)), dma((1,)),
        dma((2,)), dma((2,)),
        dma((2,)), dma((2,)),
    ]
    return pl.pallas_call(
        kernel,
        out_shape=jax.ShapeDtypeStruct((TOK, COLS), BF),
        in_specs=[anyw, vmem, vmem, anyw, anyw, anyw],
        out_specs=vmem,
        scratch_shapes=scratch,
        compiler_params=pltpu.CompilerParams(
            collective_id=0, has_side_effects=True, vmem_limit_bytes=56 * 1024 * 1024
        ),
    )(hidden, norm_gain.reshape(1, D), freq, wq, wkv, wo)


def solution(mesh):
    spec = P("row", "col")
    return jax.shard_map(
        per_device, mesh=mesh, in_specs=(spec, P(), spec, spec, spec, spec), out_specs=spec, check_vma=False
    )
```
